32 devices in a mesh: section: 4 (over z), dp: 8 (over y, x, core).
Axes of the slice: x: 2, y: 2, z: 4, core: 2. Of those that a mesh axis runs over, the one named last changes fastest.
Arguments:
- feed_down: bfloat16 [4, 512, 4096], P('section', 'dp'), may hold values from -6 to 6
- feed_up: bfloat16 [4, 512, 4096], P('section', 'dp'), may hold values from -6 to 6
- cotangent_down: bfloat16 [4, 512, 4096], P('section', 'dp'), may hold values from -6 to 6
- cotangent_up: bfloat16 [4, 512, 4096], P('section', 'dp'), may hold values from -6 to 6
- roster: int32 [4, 2, 2], P('section'), may hold values from 0 to 1, each once within a row
- value_weight: bfloat16 [4, 4096, 512], P('section'), may hold values from -0.09375 to 0.09375
Outputs:
- next_down: bfloat16 [4, 512, 4096], P('section', 'dp')
- next_up: bfloat16 [4, 512, 4096], P('section', 'dp')
- back_down: bfloat16 [4, 512, 4096], P('section', 'dp')
- back_up: bfloat16 [4, 512, 4096], P('section', 'dp')
- grad_weight: float32 [4, 4096, 512], P('section', 'dp')
The draws below stay inside these ranges and needn't reach their ends.
Inputs may be any that keep to these rules, and one draw needn't show every extreme that they name: roster[s, 0, :] and roster[s, 1, :] are each a permutation of the 2 micro-batches: block j of the cotangents that section index s receives for a leg belongs to micro-batch roster[s, leg, j].
All inputs are finite; a program needn't handle non-finite values.
Results may differ from the reference program's by a relative error of at most 0.005.
Values may be sent and summed in bfloat16 or wider, within the bound.
No kernel may reach another device: no remote copies, remote signals or barrier semaphores. Data moves between devices by JAX's collectives and lax.ppermute only.
A program may use at most 64 MiB of HBM per device.

```python
import jax
import jax.numpy as jnp
from jax import lax

D = 4096
KVH = 4
HD = 128
GROUPS = 8
MB = 2
RM = 32
TOKS = 512
N_SECTION = 4
N_DP = 8


def steps_of(own_key, dims, split, smallest, largest):
    level, own = 1.0, jax.random.fold_in(own_key, 6)
    for axis_at, shards_of in split:
        steps = jnp.exp(jax.random.uniform(jax.random.fold_in(own, axis_at), (shards_of,), jnp.float32, smallest / len(split), largest / len(split)))
        level = level * jnp.repeat(steps, dims[axis_at] // shards_of).reshape([-1 if axis == axis_at else 1 for axis in range(len(dims))])
    return level


def bell_draw(rng, shape, scale, bound, split=(), held_as=jnp.bfloat16):
    gain = steps_of(rng, shape, split, -0.22, 0.18) if split else 1.0
    array = jax.random.normal(rng, shape, jnp.float32) * scale * gain
    return jnp.minimum(jnp.maximum(array, -bound), bound).astype(held_as)


def setup_inputs(seed: int = 0) -> dict:
    key_list = jax.random.split(jax.random.key(seed), 7)
    feed_down = bell_draw(key_list[0], (N_SECTION, TOKS, D), 1.0, 6.0, ((0, 4), (1, 8)))
    feed_up = bell_draw(key_list[1], (N_SECTION, TOKS, D), 1.0, 6.0, ((0, 4), (1, 8)))
    cotangent_down = bell_draw(key_list[2], (N_SECTION, TOKS, D), 1.0, 6.0, ((0, 4), (1, 8)))
    cotangent_up = bell_draw(key_list[3], (N_SECTION, TOKS, D), 1.0, 6.0, ((0, 4), (1, 8)))
    roster = jax.vmap(lambda own: jax.random.permutation(own, MB))(jax.random.split(key_list[4], N_SECTION * 2)).reshape((N_SECTION, 2, MB)).astype(jnp.int32)
    value_weight = bell_draw(key_list[5], (N_SECTION, D, KVH * HD), D ** -0.5, 0.09375, ((0, 4),))
    return dict(feed_down=feed_down, feed_up=feed_up, cotangent_down=cotangent_down, cotangent_up=cotangent_up, roster=roster, value_weight=value_weight)


EPSILON = 1e-05

def normalize(inputs):
    values = inputs.astype(jnp.float32)
    inverse = lax.rsqrt(lax.optimization_barrier(jnp.mean(values * values, axis=-1, keepdims=True)) + EPSILON)
    return (values * inverse, inverse)

def arrange(received, roster_row, devices):
    blocks = roster_row.shape[0]
    match_table = (roster_row[:, None] == jnp.arange(blocks, dtype=jnp.int32)[None, :]).astype(jnp.float32)
    shaped = received.reshape(devices, blocks, -1).astype(jnp.float32)
    placed = jnp.einsum('pjx,jm->pmx', shaped, match_table)
    return placed.astype(jnp.bfloat16).reshape(received.shape)

def one_leg(inputs, grads, weight):
    scaled, inverse = normalize(inputs)
    normed = scaled.astype(jnp.bfloat16)
    values = jnp.dot(normed, weight, preferred_element_type=jnp.float32)
    row_total = inputs.shape[0]
    spread = jnp.broadcast_to(values.reshape(row_total, KVH, 1, HD), (row_total, KVH, GROUPS, HD)).reshape(row_total, -1)
    advanced = (inputs.astype(jnp.float32) + spread).astype(jnp.bfloat16)
    grouped = lax.optimization_barrier(jnp.sum(grads.astype(jnp.float32).reshape(row_total, KVH, GROUPS, HD), axis=2)).reshape(row_total, -1).astype(jnp.bfloat16)
    back_norm = jnp.dot(grouped, weight.T, preferred_element_type=jnp.float32)
    through = inverse * (back_norm - scaled * lax.optimization_barrier(jnp.mean(back_norm * scaled, axis=-1, keepdims=True)))
    behind = (grads.astype(jnp.float32) + through).astype(jnp.bfloat16)
    return (advanced, behind, normed, grouped)

def reference(feed_down, feed_up, cotangent_down, cotangent_up, roster, value_weight):
    sections = feed_down.shape[0]
    factor = float(2 * MB * RM * N_DP) ** (-0.5)

    def per_section(section_index):
        lower_index = (section_index - 1) % sections
        upper_index = (section_index + 1) % sections
        weight = value_weight[section_index]
        grads_down = arrange(cotangent_down[upper_index], roster[section_index, 0], N_DP)
        grads_up = arrange(cotangent_up[lower_index], roster[section_index, 1], N_DP)
        advanced_down, behind_down, normed_down, grouped_down = one_leg(feed_down[lower_index], grads_down, weight)
        advanced_up, behind_up, normed_up, grouped_up = one_leg(feed_up[upper_index], grads_up, weight)
        normed_all = jnp.concatenate([normed_down, normed_up], axis=0)
        grouped_all = jnp.concatenate([grouped_down, grouped_up], axis=0)
        total = jnp.dot(normed_all.T, grouped_all, preferred_element_type=jnp.float32)
        return (advanced_down, advanced_up, behind_down, behind_up, total * factor)
    next_down, next_up, back_down, back_up, grad_weight = lax.map(per_section, jnp.arange(sections, dtype=jnp.int32))
    return (next_down, next_up, back_down, back_up, grad_weight)
```

```python
import functools

import jax
import jax.numpy as jnp
from jax import lax
from jax.experimental import pallas as pl
from jax.experimental.pallas import tpu as pltpu
from jax.sharding import PartitionSpec as P


KVH = 4
HD = 128
GROUPS = 8


EPSILON = 1e-05


MIB = 2**20


def passed_along(shard, axis, by):
    count = lax.axis_size(axis)
    return lax.ppermute(shard, axis, [(i, (i + by) % count) for i in range(count)])


def whole_vmem():
    return pl.BlockSpec(memory_space=pltpu.VMEM)


def group_kernel(down_ref, up_ref, down_out, up_out):
    for src, dst in ((down_ref, down_out), (up_ref, up_out)):
        for k in range(KVH):
            total = src[:, k * GROUPS * HD : (k * GROUPS + 1) * HD].astype(jnp.float32)
            for j in range(1, GROUPS):
                at = (k * GROUPS + j) * HD
                total = total + src[:, at : at + HD].astype(jnp.float32)
            dst[:, k * HD : (k + 1) * HD] = total.astype(dst.dtype)


def group_sums(down, up):
    rows, width = down.shape
    step = rows // 2
    wide = pl.BlockSpec((step, width), lambda i: (i, 0))
    narrow = pl.BlockSpec((step, width // GROUPS), lambda i: (i, 0))
    out = jax.ShapeDtypeStruct((rows, width // GROUPS), down.dtype)
    return pl.pallas_call(
        group_kernel,
        grid=(rows // step,),
        in_specs=[wide, wide],
        out_specs=[narrow, narrow],
        out_shape=[out, out],
        name="group_sums",
        compiler_params=pltpu.CompilerParams(vmem_limit_bytes=6 * MIB),
        cost_estimate=pl.CostEstimate(
            flops=2 * rows * width, bytes_accessed=4 * rows * width, transcendentals=0
        ),
    )(down, up)


def normalize_kernel(members, x_ref, out_ref):
    x = x_ref[...].astype(jnp.float32)
    inverse = lax.rsqrt(jnp.mean(x * x, axis=-1, keepdims=True) + EPSILON)
    width = x.shape[1] // members
    for p in range(members):
        part = x_ref[:, p * width : (p + 1) * width].astype(jnp.float32)
        out_ref[p] = (part * inverse).astype(out_ref.dtype)


def normalized_slices(x, members):
    rows, width = x.shape
    return pl.pallas_call(
        functools.partial(normalize_kernel, members),
        in_specs=[whole_vmem()],
        out_specs=whole_vmem(),
        out_shape=jax.ShapeDtypeStruct((members, rows, width // members), x.dtype),
        name="normalized_slices",
        compiler_params=pltpu.CompilerParams(vmem_limit_bytes=4 * MIB),
        cost_estimate=pl.CostEstimate(
            flops=4 * rows * width, bytes_accessed=4 * rows * width, transcendentals=rows
        ),
    )(x)


def span_kernel(
    down_ref, up_ref, grouped_ref, weight_ref,
    next_down, next_up, through_down, through_up,
    scaled, normed, back, values, inner,
):
    step = pl.program_id(0)
    rows = down_ref.shape[0]
    tile = weight_ref.shape[0]

    @pl.when(step == 0)
    def _():
        values[...] = jnp.zeros_like(values)
        inner[...] = jnp.zeros_like(inner)
        for leg, ref in enumerate((down_ref, up_ref)):
            x = ref[...].astype(jnp.float32)
            inverse = lax.rsqrt(jnp.mean(x * x, axis=-1, keepdims=True) + EPSILON)
            own = slice(leg * rows, (leg + 1) * rows)
            scaled[own, :] = x * inverse
            normed[own, :] = (x * inverse).astype(normed.dtype)

    columns = pl.ds(pl.multiple_of(step * tile, tile), tile)
    weight = weight_ref[...]
    values[...] += jnp.dot(normed[:, columns], weight, preferred_element_type=jnp.float32)
    part = lax.dot_general(
        grouped_ref[...], weight, (((1,), (1,)), ((), ())), preferred_element_type=jnp.float32
    )
    back[:, columns] = part
    inner[...] += jnp.sum(part * scaled[:, columns], axis=-1, keepdims=True)

    @pl.when(step == pl.num_programs(0) - 1)
    def _():
        width = down_ref.shape[1]
        for leg, (ref, nxt, thr) in enumerate(
            ((down_ref, next_down, through_down), (up_ref, next_up, through_up))
        ):
            own = slice(leg * rows, (leg + 1) * rows)
            x = ref[...].astype(jnp.float32)
            inverse = lax.rsqrt(jnp.mean(x * x, axis=-1, keepdims=True) + EPSILON)
            mean = inner[own, :] * (1.0 / width)
            for c in range(width // HD):
                at = slice(c * HD, (c + 1) * HD)
                k = c // GROUPS
                nxt[:, at] = (
                    ref[:, at].astype(jnp.float32) + values[own, k * HD : (k + 1) * HD]
                ).astype(nxt.dtype)
                thr[:, at] = inverse * (back[own, at] - scaled[own, at] * mean)


def span(down, up, grouped, weight):
    rows, width = down.shape
    inner = weight.shape[1]
    tile = 512 if width % 512 == 0 else width
    whole = pl.BlockSpec((rows, width), lambda i: (0, 0))
    return pl.pallas_call(
        span_kernel,
        grid=(width // tile,),
        in_specs=[
            whole_vmem(),
            whole_vmem(),
            whole_vmem(),
            pl.BlockSpec((tile, inner), lambda i: (i, 0)),
        ],
        out_specs=[whole, whole, whole_vmem(), whole_vmem()],
        out_shape=[jax.ShapeDtypeStruct((rows, width), down.dtype)] * 2
        + [jax.ShapeDtypeStruct((rows, width), jnp.float32)] * 2,
        scratch_shapes=[
            pltpu.VMEM((2 * rows, width), jnp.float32),
            pltpu.VMEM((2 * rows, width), down.dtype),
            pltpu.VMEM((2 * rows, width), jnp.float32),
            pltpu.VMEM((2 * rows, inner), jnp.float32),
            pltpu.VMEM((2 * rows, 1), jnp.float32),
        ],
        compiler_params=pltpu.CompilerParams(vmem_limit_bytes=24 * MIB),
        name="span",
        cost_estimate=pl.CostEstimate(
            flops=8 * rows * width * inner,
            bytes_accessed=2 * width * inner + 16 * rows * width,
            transcendentals=2 * rows,
        ),
    )(down, up, grouped, weight)


def weight_kernel(factor, me_ref, down_ref, up_ref, own_ref, other_ref, out_ref):
    chips = own_ref.shape[0]
    chip = me_ref[0] // 2
    core = me_ref[0] % 2
    total = jnp.zeros(out_ref.shape, jnp.float32)
    over_tokens = (((0,), (0,)), ((), ()))
    for c in range(chips):
        same = (chip ^ c) * 2 + core
        other = (chip ^ c) * 2 + 1 - core
        normed = jnp.concatenate(
            [down_ref[same], up_ref[same], down_ref[other], up_ref[other]], axis=0
        )
        grouped = jnp.concatenate([own_ref[c], other_ref[c]], axis=0)
        total = total + lax.dot_general(
            normed, grouped, over_tokens, preferred_element_type=jnp.float32
        )
    out_ref[...] = total * factor


def weight_gradient(normed_down, normed_up, own, other, me, factor):
    members, rows, width = normed_down.shape
    inner = own.shape[-1]
    return pl.pallas_call(
        functools.partial(weight_kernel, factor),
        in_specs=[pl.BlockSpec(memory_space=pltpu.SMEM)] + [whole_vmem()] * 4,
        out_specs=whole_vmem(),
        out_shape=jax.ShapeDtypeStruct((width, inner), jnp.float32),
        name="weight_gradient",
        compiler_params=pltpu.CompilerParams(vmem_limit_bytes=16 * MIB),
        cost_estimate=pl.CostEstimate(
            flops=4 * members * rows * width * inner,
            bytes_accessed=4 * members * rows * (width + inner) + 4 * width * inner,
            transcendentals=0,
        ),
    )(me, normed_down, normed_up, own, other)


def chosen_blocks(blocks_ref, match_ref, m):
    chosen = blocks_ref[0].astype(jnp.float32)
    for j in range(1, blocks_ref.shape[0]):
        mine = match_ref[m, j : j + 1, 0:1] != 0
        chosen = jnp.where(mine, blocks_ref[j].astype(jnp.float32), chosen)
    return chosen


def arrange_kernel(match_down, match_up, down_ref, up_ref, out_ref):
    blocks, rows, _ = down_ref.shape
    for leg, (match, ref) in enumerate(((match_down, down_ref), (match_up, up_ref))):
        for m in range(blocks):
            at = (leg * blocks + m) * rows
            out_ref[at : at + rows, :] = chosen_blocks(ref, match, m).astype(out_ref.dtype)


def arranged_sums(down, up, match_down, match_up):
    rows, width = down.shape
    blocks = match_down.shape[0]
    return pl.pallas_call(
        arrange_kernel,
        in_specs=[whole_vmem()] * 4,
        out_specs=whole_vmem(),
        out_shape=jax.ShapeDtypeStruct((2 * rows, width), down.dtype),
        name="arranged_sums",
        compiler_params=pltpu.CompilerParams(vmem_limit_bytes=4 * MIB),
        cost_estimate=pl.CostEstimate(
            flops=4 * rows * width, bytes_accessed=8 * rows * width, transcendentals=0
        ),
    )(
        match_down,
        match_up,
        down.reshape(blocks, rows // blocks, width),
        up.reshape(blocks, rows // blocks, width),
    )


def finish_kernel(match_ref, raw_ref, through_ref, out_ref):
    m = pl.program_id(0)
    total = chosen_blocks(raw_ref, match_ref, m) + through_ref[m]
    out_ref[0] = total.astype(out_ref.dtype)


def finished(raw, match, through):
    rows, width = raw.shape
    blocks = match.shape[0]
    cut = (blocks, rows // blocks, width)
    return pl.pallas_call(
        finish_kernel,
        grid=(blocks,),
        in_specs=[whole_vmem()] * 3,
        out_specs=pl.BlockSpec((1,) + cut[1:], lambda m: (m, 0, 0)),
        out_shape=jax.ShapeDtypeStruct(cut, raw.dtype),
        name="finished",
        compiler_params=pltpu.CompilerParams(vmem_limit_bytes=4 * MIB),
        cost_estimate=pl.CostEstimate(
            flops=2 * rows * width, bytes_accessed=8 * rows * width, transcendentals=0
        ),
    )(match, raw.reshape(cut), through.reshape(cut)).reshape(rows, width)


def matches(roster_row):
    blocks = roster_row.shape[0]
    wanted = jnp.arange(blocks, dtype=jnp.int32)
    equal = (roster_row[None, :] == wanted[:, None]).astype(jnp.int32)
    return jnp.broadcast_to(equal[:, :, None], (blocks, blocks, HD))


def on_device(feed_down, feed_up, cotangent_down, cotangent_up, roster, value_weight):
    members = lax.axis_size("dp")
    chips = members // 2
    me = lax.axis_index("dp")
    weight = value_weight[0]
    rows = feed_down.shape[1]
    sums_down, sums_up = group_sums(cotangent_down[0], cotangent_up[0])

    x_down = passed_along(feed_down[0], "section", 1)
    sums_up = passed_along(sums_up, "section", 1)
    sums_down = passed_along(sums_down, "section", -1)
    x_up = passed_along(feed_up[0], "section", -1)
    raw_up = passed_along(cotangent_up[0], "section", 1)
    raw_down = passed_along(cotangent_down[0], "section", -1)

    match_down = matches(roster[0, 0])
    match_up = matches(roster[0, 1])
    grouped = arranged_sums(sums_down, sums_up, match_down, match_up)

    def exchanged(slices):
        return lax.all_to_all(slices, "dp", split_axis=0, concat_axis=0, tiled=True)

    normed_down = exchanged(normalized_slices(x_down, members))
    normed_up = exchanged(normalized_slices(x_up, members))

    pieces = [grouped]
    for c in range(1, chips):
        pieces.append(
            lax.ppermute(grouped, "dp", [(i, (((i // 2) ^ c) * 2) + i % 2) for i in range(members)])
        )
    own = jnp.stack(pieces)
    other = lax.ppermute(own, "dp", [(i, i ^ 1) for i in range(members)])

    next_down, next_up, through_down, through_up = span(x_down, x_up, grouped, weight)

    factor = float(2 * rows * members) ** (-0.5)
    summed = weight_gradient(
        normed_down, normed_up, own, other, me.reshape(1).astype(jnp.int32), factor
    )

    back_down = finished(raw_down, match_down, through_down)
    back_up = finished(raw_up, match_up, through_up)
    return (
        next_down[None],
        next_up[None],
        back_down[None],
        back_up[None],
        summed[None],
    )


def solution(mesh):
    placed = (
        P("section", "dp", None),
        P("section", "dp", None),
        P("section", "dp", None),
        P("section", "dp", None),
        P("section", None, None),
        P("section", None, None),
    )
    return jax.shard_map(
        on_device,
        mesh=mesh,
        in_specs=placed,
        out_specs=(
            P("section", "dp", None),
            P("section", "dp", None),
            P("section", "dp", None),
            P("section", "dp", None),
            P("section", "dp", None),
        ),
        check_vma=False,
    )
```

```python
import functools
import math

import jax
import jax.numpy as jnp
from jax import lax
from jax.experimental import pallas as pl
from jax.experimental.pallas import tpu as pltpu
from jax.sharding import PartitionSpec as P


KVH = 4
HD = 128
GROUPS = 8


EPSILON = 1e-05


MIB = 2**20


def passed_along(shard, axis, by):
    count = lax.axis_size(axis)
    return lax.ppermute(shard, axis, [(i, (i + by) % count) for i in range(count)])


def whole_vmem():
    return pl.BlockSpec(memory_space=pltpu.VMEM)


def called(kernel, operands, outputs, scratch=(), flops=0, vmem=4, **more):
    moved = sum(x.size * x.dtype.itemsize for x in list(operands) + list(outputs))
    return pl.pallas_call(
        kernel,
        in_specs=more.get("in_specs", [whole_vmem()] * len(operands)),
        out_specs=[whole_vmem()] * len(outputs),
        out_shape=list(outputs),
        scratch_shapes=list(scratch),
        compiler_params=pltpu.CompilerParams(vmem_limit_bytes=vmem * MIB),
        cost_estimate=pl.CostEstimate(
            flops=flops, bytes_accessed=moved, transcendentals=0
        ),
    )(*operands)


def group_kernel(down_ref, up_ref, down_out, up_out, first_out, rest_out):
    step = pl.program_id(0)
    for src, dst in ((down_ref, down_out), (up_ref, up_out)):
        for k in range(KVH):
            total = src[:, k * GROUPS * HD : (k * GROUPS + 1) * HD].astype(jnp.float32)
            for j in range(1, GROUPS):
                at = (k * GROUPS + j) * HD
                total = total + src[:, at : at + HD].astype(jnp.float32)
            dst[:, k * HD : (k + 1) * HD] = total.astype(dst.dtype)

    @pl.when(step == 0)
    def _():
        first_out[...] = down_ref[...]

    @pl.when(step > 0)
    def _():
        rest_out[...] = down_ref[...]


def group_sums(down, up):
    rows, width = down.shape
    steps = 4
    step = rows // steps
    wide = pl.BlockSpec((step, width), lambda i: (i, 0))
    narrow = pl.BlockSpec((step, width // GROUPS), lambda i: (i, 0))
    out = jax.ShapeDtypeStruct((rows, width // GROUPS), down.dtype)
    return pl.pallas_call(
        group_kernel,
        grid=(steps,),
        in_specs=[wide, wide],
        out_specs=[
            narrow,
            narrow,
            pl.BlockSpec((step, width), lambda i: (0, 0)),
            pl.BlockSpec((step, width), lambda i: (jnp.maximum(i - 1, 0), 0)),
        ],
        out_shape=[
            out,
            out,
            jax.ShapeDtypeStruct((step, width), down.dtype),
            jax.ShapeDtypeStruct((rows - step, width), down.dtype),
        ],
        name="group_sums",
        compiler_params=pltpu.CompilerParams(vmem_limit_bytes=6 * MIB),
        cost_estimate=pl.CostEstimate(
            flops=2 * rows * width, bytes_accessed=6 * rows * width, transcendentals=0
        ),
    )(down, up)


def inverse_of(x):
    return lax.rsqrt(jnp.mean(x * x, axis=-1, keepdims=True) + EPSILON)


def unit_of(width, members, inner):
    return math.gcd(width // members, inner)


def write_normed(chips, x_ref, piece_refs):
    inverse = inverse_of(x_ref[...].astype(jnp.float32))
    unit = piece_refs[0].shape[-1]
    per_chip = x_ref.shape[1] // chips
    chip = lax.axis_index("dp") // 2
    for c, piece in enumerate(piece_refs):
        base = (chip ^ c) * per_chip
        for b in range(per_chip // unit):
            at = pl.ds(pl.multiple_of(base + b * unit, unit), unit)
            piece[b] = (x_ref[:, at].astype(jnp.float32) * inverse).astype(piece.dtype)


def down_kernel(chips, x_ref, match_down, match_up, down_ref, up_ref, grouped_ref, *pieces):
    write_normed(chips, x_ref, pieces)
    blocks, rows, inner = down_ref.shape
    unit = pieces[0].shape[-1]
    own = x_ref.shape[1] // chips // unit
    for leg, (match, ref) in enumerate(((match_down, down_ref), (match_up, up_ref))):
        for m in range(blocks):
            chosen = ref[0].astype(jnp.float32)
            for j in range(1, blocks):
                mine = match[m, j : j + 1, 0:1] != 0
                chosen = jnp.where(mine, ref[j].astype(jnp.float32), chosen)
            chosen = chosen.astype(grouped_ref.dtype)
            at = (leg * blocks + m) * rows
            grouped_ref[at : at + rows, :] = chosen
            for piece in pieces:
                for b in range(inner // unit):
                    piece[own + leg * (inner // unit) + b, m * rows : (m + 1) * rows, :] = chosen[
                        :, b * unit : (b + 1) * unit
                    ]


def up_kernel(chips, x_ref, *pieces):
    write_normed(chips, x_ref, pieces)


def pieces_down(x, sums_down, sums_up, match_down, match_up, members):
    rows, width = x.shape
    inner = sums_down.shape[1]
    chips = members // 2
    unit = unit_of(width, members, inner)
    count = width // chips // unit + 2 * inner // unit
    blocks = match_down.shape[0]
    cut = (blocks, rows // blocks, inner)
    outputs = [jax.ShapeDtypeStruct((2 * rows, inner), x.dtype)]
    outputs += [jax.ShapeDtypeStruct((count, rows, unit), x.dtype)] * chips
    return called(
        functools.partial(down_kernel, chips),
        (x, match_down, match_up, sums_down.reshape(cut), sums_up.reshape(cut)),
        outputs,
        flops=4 * rows * width,
    )


def pieces_up(x, inner, members):
    rows, width = x.shape
    chips = members // 2
    unit = unit_of(width, members, inner)
    outputs = [jax.ShapeDtypeStruct((width // chips // unit, rows, unit), x.dtype)] * chips
    return called(functools.partial(up_kernel, chips), (x,), outputs, flops=4 * rows * width)


def product_kernel(chips, inner, *refs):
    down, up = refs[:chips], refs[chips : 2 * chips]
    keep_ref, send_ref = refs[2 * chips :]
    unit = down[0].shape[-1]
    half = keep_ref.shape[0] // unit
    own = 2 * half
    core = lax.axis_index("dp") % 2
    over_tokens = (((0,), (0,)), ((), ()))

    def stacked(at, grouped):
        legs = [ref[at[0]] for ref in down]
        legs += [ref[at[1]] for ref in (down if grouped else up)]
        return jnp.concatenate(legs, axis=0)

    for g in range(inner // unit):
        grouped = stacked((own + g, own + inner // unit + g), True)
        for dest, out_ref in ((core, keep_ref), (1 - core, send_ref)):
            for b in range(half):
                at = dest * half + b
                out_ref[b * unit : (b + 1) * unit, g * unit : (g + 1) * unit] = lax.dot_general(
                    stacked((at, at), False),
                    grouped,
                    over_tokens,
                    preferred_element_type=jnp.float32,
                )


def products(down, up, width, inner, members):
    chips = members // 2
    rows = up[0].shape[1]
    out = jax.ShapeDtypeStruct((width // members, inner), jnp.float32)
    return called(
        functools.partial(product_kernel, chips, inner),
        (*down, *up),
        [out, out],
        flops=8 * chips * rows * (width // members) * inner,
        vmem=8,
    )


def combine_kernel(factor, keep_ref, got_ref, out_ref):
    out_ref[...] = (keep_ref[...] + got_ref[...]) * factor


def combined(keep, got, factor):
    rows, inner = keep.shape
    step = rows // 2
    part = pl.BlockSpec((step, inner), lambda i: (i, 0))
    return pl.pallas_call(
        functools.partial(combine_kernel, factor),
        grid=(rows // step,),
        in_specs=[part, part],
        out_specs=part,
        out_shape=jax.ShapeDtypeStruct(keep.shape, keep.dtype),
        name="combine",
        compiler_params=pltpu.CompilerParams(vmem_limit_bytes=4 * MIB),
        cost_estimate=pl.CostEstimate(
            flops=2 * rows * inner, bytes_accessed=12 * rows * inner, transcendentals=0
        ),
    )(keep, got)


def span_kernel(
    down_ref, up_ref, grouped_ref, weight_ref,
    next_down, next_up, through,
    scaled, back, held, arrived,
):
    rows, width = down_ref.shape
    tiles, tile, inner = held.shape
    copies = [
        pltpu.make_async_copy(weight_ref.at[pl.ds(t * tile, tile), :], held.at[t], arrived.at[t])
        for t in range(tiles)
    ]
    for copy in copies:
        copy.start()
    inverses = []
    for leg, ref in enumerate((down_ref, up_ref)):
        x = ref[...].astype(jnp.float32)
        inverse = inverse_of(x)
        inverses.append(inverse)
        scaled[leg * rows : (leg + 1) * rows, :] = x * inverse
    values = jnp.zeros((2 * rows, inner), jnp.float32)
    total = jnp.zeros((2 * rows, HD), jnp.float32)
    grouped = grouped_ref[...]
    for t, copy in enumerate(copies):
        copy.wait()
        weight = held[t]
        at = slice(t * tile, (t + 1) * tile)
        normed = scaled[:, at].astype(down_ref.dtype)
        values = values + jnp.dot(normed, weight, preferred_element_type=jnp.float32)
        part = lax.dot_general(
            grouped, weight, (((1,), (1,)), ((), ())), preferred_element_type=jnp.float32
        )
        back[:, at] = part
        for c in range(tile // HD):
            lanes = slice(c * HD, (c + 1) * HD)
            total = total + part[:, lanes] * scaled[:, t * tile + c * HD : t * tile + (c + 1) * HD]
    means = jnp.sum(total, axis=-1, keepdims=True) * (1.0 / width)
    for leg, (ref, nxt) in enumerate(((down_ref, next_down), (up_ref, next_up))):
        own = slice(leg * rows, (leg + 1) * rows)
        mean = jnp.broadcast_to(means[own], (rows, HD))
        inverse = jnp.broadcast_to(inverses[leg], (rows, HD))
        for k in range(KVH):
            spread = values[own, k * HD : (k + 1) * HD]
            for j in range(GROUPS):
                at = slice((k * GROUPS + j) * HD, (k * GROUPS + j + 1) * HD)
                nxt[:, at] = (ref[:, at].astype(jnp.float32) + spread).astype(nxt.dtype)
                through[leg, :, at] = inverse * (back[own, at] - scaled[own, at] * mean)


def span(down, up, grouped, weight):
    rows, width = down.shape
    inner = weight.shape[1]
    tile = math.gcd(width, 512)
    return called(
        span_kernel,
        (down, up, grouped, weight),
        [jax.ShapeDtypeStruct((rows, width), down.dtype)] * 2
        + [jax.ShapeDtypeStruct((2, rows, width), jnp.float32)],
        scratch=[
            pltpu.VMEM((2 * rows, width), jnp.float32),
            pltpu.VMEM((2 * rows, width), jnp.float32),
            pltpu.VMEM((width // tile, tile, inner), weight.dtype),
            pltpu.SemaphoreType.DMA((width // tile,)),
        ],
        flops=8 * rows * width * inner,
        vmem=12,
        in_specs=[whole_vmem()] * 3 + [pl.BlockSpec(memory_space=pltpu.HBM)],
    )


def finish_kernel(leg, cuts, match_ref, through_ref, *refs):
    pieces, out_ref = refs[:-1], refs[-1]
    blocks, rows, _ = out_ref.shape
    unit = functools.reduce(math.gcd, cuts, rows)

    def units(start):
        at = 0
        for ref, cut in zip(pieces, cuts):
            if start < at + cut:
                return ref[start - at : start - at + unit, :]
            at += cut

    for m in range(blocks):
        for start in range(0, rows, unit):
            chosen = units(start).astype(jnp.float32)
            for j in range(1, blocks):
                mine = match_ref[m, j : j + 1, 0:1] != 0
                chosen = jnp.where(mine, units(j * rows + start).astype(jnp.float32), chosen)
            at = m * rows + start
            total = chosen + through_ref[leg, at : at + unit, :]
            out_ref[m, start : start + unit, :] = total.astype(out_ref.dtype)


def finished(pieces, match, through, leg):
    width = pieces[0].shape[1]
    cuts = [piece.shape[0] for piece in pieces]
    rows = sum(cuts)
    blocks = match.shape[0]
    cut = (blocks, rows // blocks, width)
    (out,) = called(
        functools.partial(finish_kernel, leg, cuts),
        (match, through, *pieces),
        [jax.ShapeDtypeStruct(cut, pieces[0].dtype)],
        flops=2 * rows * width,
    )
    return out.reshape(rows, width)


def matches(roster_row):
    blocks = roster_row.shape[0]
    wanted = jnp.arange(blocks, dtype=jnp.int32)
    equal = (roster_row[None, :] == wanted[:, None]).astype(jnp.int32)
    return jnp.broadcast_to(equal[:, :, None], (blocks, blocks, HD))


def on_device(feed_down, feed_up, cotangent_down, cotangent_up, roster, value_weight):
    members = lax.axis_size("dp")
    chips = members // 2
    weight = value_weight[0]
    rows, width = feed_down.shape[1:]
    inner = weight.shape[1]
    match_down = matches(roster[0, 0])
    match_up = matches(roster[0, 1])

    sums_down, sums_up, first_down, rest_down = group_sums(cotangent_down[0], cotangent_up[0])
    x_down = passed_along(feed_down[0], "section", 1)
    sums_up = passed_along(sums_up, "section", 1)
    sums_down = passed_along(sums_down, "section", -1)
    x_up = passed_along(feed_up[0], "section", -1)
    raw_down = [passed_along(first_down, "section", -1), passed_along(rest_down, "section", -1)]
    raw_up = [passed_along(cotangent_up[0], "section", 1)]

    def exchanged(pieces):
        got = [pieces[0]]
        for c in range(1, chips):
            to = [(i, ((i // 2) ^ c) * 2 + i % 2) for i in range(members)]
            got.append(lax.ppermute(pieces[c], "dp", to))
        return got

    grouped, *sent_down = pieces_down(x_down, sums_down, sums_up, match_down, match_up, members)
    got_down = exchanged(sent_down)
    got_up = exchanged(pieces_up(x_up, inner, members))

    next_down, next_up, through = span(x_down, x_up, grouped, weight)

    keep, send = products(got_down, got_up, width, inner, members)
    got = lax.ppermute(send, "dp", [(i, i ^ 1) for i in range(members)])
    summed = combined(keep, got, float(2 * rows * members) ** (-0.5))

    back_down = finished(raw_down, match_down, through, 0)
    back_up = finished(raw_up, match_up, through, 1)
    return (
        next_down[None],
        next_up[None],
        back_down[None],
        back_up[None],
        summed[None],
    )


def solution(mesh):
    rows = P("section", "dp", None)
    kept = P("section", None, None)
    return jax.shard_map(
        on_device,
        mesh=mesh,
        in_specs=(rows, rows, rows, rows, kept, kept),
        out_specs=(rows, rows, rows, rows, rows),
        check_vma=False,
    )
```

```python
import functools
import math

import jax
import jax.numpy as jnp
from jax import lax
from jax.experimental import pallas as pl
from jax.experimental.pallas import tpu as pltpu
from jax.sharding import PartitionSpec as P


KVH = 4
HD = 128
GROUPS = 8


EPSILON = 1e-05


MIB = 2**20


def passed_along(shard, axis, by):
    count = lax.axis_size(axis)
    return lax.ppermute(shard, axis, [(i, (i + by) % count) for i in range(count)])


def whole_vmem():
    return pl.BlockSpec(memory_space=pltpu.VMEM)


def called(kernel, operands, outputs, scratch=(), flops=0, vmem=4, **more):
    moved = sum(x.size * x.dtype.itemsize for x in list(operands) + list(outputs))
    return pl.pallas_call(
        kernel,
        in_specs=more.get("in_specs", [whole_vmem()] * len(operands)),
        out_specs=[whole_vmem()] * len(outputs),
        out_shape=list(outputs),
        scratch_shapes=list(scratch),
        compiler_params=pltpu.CompilerParams(vmem_limit_bytes=vmem * MIB),
        cost_estimate=pl.CostEstimate(
            flops=flops, bytes_accessed=moved, transcendentals=0
        ),
    )(*operands)


def group_kernel(down_ref, up_ref, down_out, up_out, *halves):
    part = pl.program_id(1)
    for src, dst in ((down_ref, down_out), (up_ref, up_out)):
        for k in range(KVH):
            total = src[:, k * GROUPS * HD : (k * GROUPS + 1) * HD].astype(jnp.float32)
            for j in range(1, GROUPS):
                at = (k * GROUPS + j) * HD
                total = total + src[:, at : at + HD].astype(jnp.float32)
            dst[:, k * HD : (k + 1) * HD] = total.astype(dst.dtype)

    for own in range(2):

        @pl.when(part == own)
        def _():
            halves[own][0] = down_ref[...]
            halves[2 + own][0] = up_ref[...]


def group_sums(down, up, blocks):
    rows, width = down.shape
    step = rows // blocks // 2
    wide = pl.BlockSpec((step, width), lambda j, i: (2 * j + i, 0))
    narrow = pl.BlockSpec((step, width // GROUPS), lambda j, i: (2 * j + i, 0))
    half = pl.BlockSpec((1, step, width), lambda j, i: (j, 0, 0))
    out = jax.ShapeDtypeStruct((rows, width // GROUPS), down.dtype)
    return pl.pallas_call(
        group_kernel,
        grid=(blocks, 2),
        in_specs=[wide, wide],
        out_specs=[narrow, narrow] + [half] * 4,
        out_shape=[out, out] + [jax.ShapeDtypeStruct((blocks, step, width), down.dtype)] * 4,
        name="group_sums",
        compiler_params=pltpu.CompilerParams(vmem_limit_bytes=6 * MIB),
        cost_estimate=pl.CostEstimate(
            flops=2 * rows * width, bytes_accessed=8 * rows * width, transcendentals=0
        ),
    )(down, up)


def inverse_of(x):
    return lax.rsqrt(jnp.mean(x * x, axis=-1, keepdims=True) + EPSILON)


def unit_of(width, members, inner):
    return math.gcd(width // members, inner)


def write_normed(chips, x_ref, piece_refs):
    inverse = inverse_of(x_ref[...].astype(jnp.float32))
    unit = piece_refs[0].shape[-1]
    per_chip = x_ref.shape[1] // chips
    chip = lax.axis_index("dp") // 2
    for c, piece in enumerate(piece_refs):
        base = (chip ^ c) * per_chip
        for b in range(per_chip // unit):
            at = pl.ds(pl.multiple_of(base + b * unit, unit), unit)
            piece[b] = (x_ref[:, at].astype(jnp.float32) * inverse).astype(piece.dtype)


def down_kernel(chips, x_ref, match_down, match_up, down_ref, up_ref, *outs):
    grouped_refs, pieces = outs[:2], outs[2:]
    write_normed(chips, x_ref, pieces)
    blocks, rows, inner = down_ref.shape
    unit = pieces[0].shape[-1]
    own = x_ref.shape[1] // chips // unit
    for leg, (match, ref) in enumerate(((match_down, down_ref), (match_up, up_ref))):
        for m in range(blocks):
            chosen = ref[0].astype(jnp.float32)
            for j in range(1, blocks):
                mine = match[m, j : j + 1, 0:1] != 0
                chosen = jnp.where(mine, ref[j].astype(jnp.float32), chosen)
            chosen = chosen.astype(x_ref.dtype)
            grouped_refs[leg][m * rows : (m + 1) * rows, :] = chosen
            for piece in pieces:
                for b in range(inner // unit):
                    piece[own + leg * (inner // unit) + b, m * rows : (m + 1) * rows, :] = chosen[
                        :, b * unit : (b + 1) * unit
                    ]


def up_kernel(chips, x_ref, *pieces):
    write_normed(chips, x_ref, pieces)


def pieces_down(x, sums_down, sums_up, match_down, match_up, members):
    rows, width = x.shape
    inner = sums_down.shape[1]
    chips = members // 2
    unit = unit_of(width, members, inner)
    count = width // chips // unit + 2 * inner // unit
    blocks = match_down.shape[0]
    cut = (blocks, rows // blocks, inner)
    outputs = [jax.ShapeDtypeStruct((rows, inner), x.dtype)] * 2
    outputs += [jax.ShapeDtypeStruct((count, rows, unit), x.dtype)] * chips
    return called(
        functools.partial(down_kernel, chips),
        (x, match_down, match_up, sums_down.reshape(cut), sums_up.reshape(cut)),
        outputs,
        flops=4 * rows * width,
    )


def pieces_up(x, inner, members):
    rows, width = x.shape
    chips = members // 2
    unit = unit_of(width, members, inner)
    outputs = [jax.ShapeDtypeStruct((width // chips // unit, rows, unit), x.dtype)] * chips
    return called(functools.partial(up_kernel, chips), (x,), outputs, flops=4 * rows * width)


def product_kernel(chips, inner, *refs):
    down, up = refs[:chips], refs[chips : 2 * chips]
    keep_ref, send_ref = refs[2 * chips :]
    unit = down[0].shape[-1]
    half = keep_ref.shape[0] // unit
    own = 2 * half
    core = lax.axis_index("dp") % 2
    over_tokens = (((0,), (0,)), ((), ()))

    def stacked(at, grouped):
        legs = [ref[at[0]] for ref in down]
        legs += [ref[at[1]] for ref in (down if grouped else up)]
        return jnp.concatenate(legs, axis=0)

    for g in range(inner // unit):
        grouped = stacked((own + g, own + inner // unit + g), True)
        for dest, out_ref in ((core, keep_ref), (1 - core, send_ref)):
            for b in range(half):
                at = dest * half + b
                out_ref[b * unit : (b + 1) * unit, g * unit : (g + 1) * unit] = lax.dot_general(
                    stacked((at, at), False),
                    grouped,
                    over_tokens,
                    preferred_element_type=jnp.float32,
                )


def products(down, up, width, inner, members):
    chips = members // 2
    rows = up[0].shape[1]
    out = jax.ShapeDtypeStruct((width // members, inner), jnp.float32)
    return called(
        functools.partial(product_kernel, chips, inner),
        (*down, *up),
        [out, out],
        flops=8 * chips * rows * (width // members) * inner,
        vmem=8,
    )


def combine_kernel(factor, keep_ref, got_ref, out_ref):
    out_ref[...] = (keep_ref[...] + got_ref[...]) * factor


def combined(keep, got, factor):
    rows, inner = keep.shape
    step = rows // 2
    part = pl.BlockSpec((step, inner), lambda i: (i, 0))
    return pl.pallas_call(
        functools.partial(combine_kernel, factor),
        grid=(rows // step,),
        in_specs=[part, part],
        out_specs=part,
        out_shape=jax.ShapeDtypeStruct(keep.shape, keep.dtype),
        name="combine",
        compiler_params=pltpu.CompilerParams(vmem_limit_bytes=4 * MIB),
        cost_estimate=pl.CostEstimate(
            flops=2 * rows * inner, bytes_accessed=12 * rows * inner, transcendentals=0
        ),
    )(keep, got)


def span_kernel(x_ref, grouped_ref, weight_ref, next_ref, through_ref, scaled, back, held, arrived):
    rows, width = x_ref.shape
    tiles, tile, inner = held.shape
    copies = [
        pltpu.make_async_copy(weight_ref.at[pl.ds(t * tile, tile), :], held.at[t], arrived.at[t])
        for t in range(tiles)
    ]
    for copy in copies:
        copy.start()
    x = x_ref[...].astype(jnp.float32)
    inverse = inverse_of(x)
    scaled[...] = x * inverse
    values = jnp.zeros((rows, inner), jnp.float32)
    total = jnp.zeros((rows, HD), jnp.float32)
    grouped = grouped_ref[...]
    for t, copy in enumerate(copies):
        copy.wait()
        weight = held[t]
        at = slice(t * tile, (t + 1) * tile)
        normed = scaled[:, at].astype(x_ref.dtype)
        values = values + jnp.dot(normed, weight, preferred_element_type=jnp.float32)
        part = lax.dot_general(
            grouped, weight, (((1,), (1,)), ((), ())), preferred_element_type=jnp.float32
        )
        back[:, at] = part
        for c in range(tile // HD):
            lanes = slice(c * HD, (c + 1) * HD)
            total = total + part[:, lanes] * scaled[:, t * tile + c * HD : t * tile + (c + 1) * HD]
    mean = jnp.sum(total, axis=-1, keepdims=True) * (1.0 / width)
    mean = jnp.broadcast_to(mean, (rows, HD))
    inverse = jnp.broadcast_to(inverse, (rows, HD))
    for k in range(KVH):
        spread = values[:, k * HD : (k + 1) * HD]
        for j in range(GROUPS):
            at = slice((k * GROUPS + j) * HD, (k * GROUPS + j + 1) * HD)
            next_ref[:, at] = (x_ref[:, at].astype(jnp.float32) + spread).astype(next_ref.dtype)
            through_ref[:, at] = inverse * (back[:, at] - scaled[:, at] * mean)


def span(x, grouped, weight):
    rows, width = x.shape
    inner = weight.shape[1]
    tile = math.gcd(width, 512)
    return called(
        span_kernel,
        (x, grouped, pltpu.with_memory_space_constraint(weight, pltpu.HBM)),
        [
            jax.ShapeDtypeStruct((rows, width), x.dtype),
            jax.ShapeDtypeStruct((rows, width), jnp.float32),
        ],
        scratch=[
            pltpu.VMEM((rows, width), jnp.float32),
            pltpu.VMEM((rows, width), jnp.float32),
            pltpu.VMEM((width // tile, tile, inner), weight.dtype),
            pltpu.SemaphoreType.DMA((width // tile,)),
        ],
        flops=4 * rows * width * inner,
        vmem=10,
        in_specs=[whole_vmem()] * 2 + [pl.BlockSpec(memory_space=pltpu.HBM)],
    )


def finish_kernel(parts, match_ref, through_ref, *refs):
    raws = refs[: len(parts)]
    out_ref, held, sent = refs[-3:]
    blocks, half, _ = raws[0].shape
    copies = []
    for i, (part, raw) in enumerate(zip(parts, raws)):
        for m in range(blocks):
            chosen = raw[0].astype(jnp.float32)
            for j in range(1, blocks):
                mine = match_ref[m, j : j + 1, 0:1] != 0
                chosen = jnp.where(mine, raw[j].astype(jnp.float32), chosen)
            at = (2 * m + part) * half
            slot = i * blocks + m
            held[slot] = (chosen + through_ref[at : at + half, :]).astype(held.dtype)
            copies.append(
                pltpu.make_async_copy(
                    held.at[slot], out_ref.at[pl.ds(at, half), :], sent.at[slot]
                )
            )
            copies[-1].start()
    for copy in copies:
        copy.wait()


def finished(raws, parts, match, through, before=None):
    rows, width = through.shape
    blocks, half, _ = raws[0].shape
    slots = blocks * len(parts)
    operands = [match, through, *raws] + ([] if before is None else [before])
    specs = [whole_vmem()] * (2 + len(raws))
    if before is not None:
        specs.append(pl.BlockSpec(memory_space=pltpu.HBM))
    return pl.pallas_call(
        functools.partial(finish_kernel, parts),
        in_specs=specs,
        out_specs=pl.BlockSpec(memory_space=pltpu.HBM),
        out_shape=jax.ShapeDtypeStruct((rows, width), raws[0].dtype),
        scratch_shapes=[
            pltpu.VMEM((slots, half, width), raws[0].dtype),
            pltpu.SemaphoreType.DMA((slots,)),
        ],
        input_output_aliases={} if before is None else {len(operands) - 1: 0},
        name="finished",
        compiler_params=pltpu.CompilerParams(vmem_limit_bytes=4 * MIB),
        cost_estimate=pl.CostEstimate(
            flops=2 * slots * half * width,
            bytes_accessed=8 * slots * half * width,
            transcendentals=0,
        ),
    )(*operands)


def matches(roster_row):
    blocks = roster_row.shape[0]
    wanted = jnp.arange(blocks, dtype=jnp.int32)
    equal = (roster_row[None, :] == wanted[:, None]).astype(jnp.int32)
    return jnp.broadcast_to(equal[:, :, None], (blocks, blocks, HD))


def on_device(feed_down, feed_up, cotangent_down, cotangent_up, roster, value_weight):
    members = lax.axis_size("dp")
    chips = members // 2
    weight = value_weight[0]
    rows, width = feed_down.shape[1:]
    inner = weight.shape[1]
    match_down = matches(roster[0, 0])
    match_up = matches(roster[0, 1])

    sums_down, sums_up, *halves = group_sums(
        cotangent_down[0], cotangent_up[0], roster.shape[2]
    )
    x_down = passed_along(feed_down[0], "section", 1)
    sums_up = passed_along(sums_up, "section", 1)
    sums_down = passed_along(sums_down, "section", -1)
    x_up = passed_along(feed_up[0], "section", -1)
    raw_down = [passed_along(half, "section", -1) for half in halves[:2]]
    raw_up = [passed_along(half, "section", 1) for half in halves[2:]]

    def exchanged(pieces):
        got = [pieces[0]]
        for c in range(1, chips):
            to = [(i, ((i // 2) ^ c) * 2 + i % 2) for i in range(members)]
            got.append(lax.ppermute(pieces[c], "dp", to))
        return got

    grouped_down, grouped_up, *sent_down = pieces_down(x_down, sums_down, sums_up, match_down, match_up, members)
    got_down = exchanged(sent_down)
    got_up = exchanged(pieces_up(x_up, inner, members))

    next_down, through_down = span(x_down, grouped_down, weight)
    next_up, through_up = span(x_up, grouped_up, weight)

    keep, send = products(got_down, got_up, width, inner, members)
    got = lax.ppermute(send, "dp", [(i, i ^ 1) for i in range(members)])
    summed = combined(keep, got, float(2 * rows * members) ** (-0.5))

    back_up = finished(raw_up, (0, 1), match_up, through_up)
    part_down = finished(raw_down[:1], (0,), match_down, through_down)
    back_down = finished(raw_down[1:], (1,), match_down, through_down, before=part_down)
    return (
        next_down[None],
        next_up[None],
        back_down[None],
        back_up[None],
        summed[None],
    )


def solution(mesh):
    rows = P("section", "dp", None)
    kept = P("section", None, None)
    return jax.shard_map(
        on_device,
        mesh=mesh,
        in_specs=(rows, rows, rows, rows, kept, kept),
        out_specs=(rows, rows, rows, rows, rows),
        check_vma=False,
    )
```

```python
import functools
import math

import jax
import jax.numpy as jnp
from jax import lax
from jax.experimental import pallas as pl
from jax.experimental.pallas import tpu as pltpu
from jax.sharding import PartitionSpec as P


KVH = 4
HD = 128
GROUPS = 8


EPSILON = 1e-05


MIB = 2**20


def passed_along(shard, axis, by):
    count = lax.axis_size(axis)
    return lax.ppermute(shard, axis, [(i, (i + by) % count) for i in range(count)])


def whole_vmem():
    return pl.BlockSpec(memory_space=pltpu.VMEM)


def called(kernel, operands, outputs, scratch=(), flops=0, vmem=4, **more):
    moved = sum(x.size * x.dtype.itemsize for x in list(operands) + list(outputs))
    return pl.pallas_call(
        kernel,
        in_specs=more.get("in_specs", [whole_vmem()] * len(operands)),
        out_specs=[whole_vmem()] * len(outputs),
        out_shape=list(outputs),
        scratch_shapes=list(scratch),
        compiler_params=pltpu.CompilerParams(vmem_limit_bytes=vmem * MIB),
        cost_estimate=pl.CostEstimate(
            flops=flops, bytes_accessed=moved, transcendentals=0
        ),
    )(*operands)


def group_kernel(down_ref, up_ref, down_out, up_out, *halves):
    part = pl.program_id(1)
    for src, dst in ((down_ref, down_out), (up_ref, up_out)):
        for k in range(KVH):
            total = src[:, k * GROUPS * HD : (k * GROUPS + 1) * HD].astype(jnp.float32)
            for j in range(1, GROUPS):
                at = (k * GROUPS + j) * HD
                total = total + src[:, at : at + HD].astype(jnp.float32)
            dst[:, k * HD : (k + 1) * HD] = total.astype(dst.dtype)

    for own in range(2):

        @pl.when(part == own)
        def _():
            halves[own][0] = up_ref[...]


def group_sums(down, up, blocks):
    rows, width = down.shape
    step = rows // blocks // 2
    wide = pl.BlockSpec((step, width), lambda j, i: (2 * j + i, 0))
    narrow = pl.BlockSpec((step, width // GROUPS), lambda j, i: (2 * j + i, 0))
    half = pl.BlockSpec((1, step, width), lambda j, i: (j, 0, 0))
    out = jax.ShapeDtypeStruct((rows, width // GROUPS), down.dtype)
    return pl.pallas_call(
        group_kernel,
        grid=(blocks, 2),
        in_specs=[wide, wide],
        out_specs=[narrow, narrow] + [half] * 2,
        out_shape=[out, out] + [jax.ShapeDtypeStruct((blocks, step, width), down.dtype)] * 2,
        name="group_sums",
        compiler_params=pltpu.CompilerParams(vmem_limit_bytes=6 * MIB),
        cost_estimate=pl.CostEstimate(
            flops=2 * rows * width, bytes_accessed=6 * rows * width, transcendentals=0
        ),
    )(down, up)


def inverse_of(x):
    return lax.rsqrt(jnp.mean(x * x, axis=-1, keepdims=True) + EPSILON)


def unit_of(width, members, inner):
    return math.gcd(width // members, inner)


def write_normed(chips, x_ref, piece_refs):
    inverse = inverse_of(x_ref[...].astype(jnp.float32))
    unit = piece_refs[0].shape[-1]
    per_chip = x_ref.shape[1] // chips
    chip = lax.axis_index("dp") // 2
    for c, piece in enumerate(piece_refs):
        base = (chip ^ c) * per_chip
        for b in range(per_chip // unit):
            at = pl.ds(pl.multiple_of(base + b * unit, unit), unit)
            piece[b] = (x_ref[:, at].astype(jnp.float32) * inverse).astype(piece.dtype)


def down_kernel(chips, x_ref, match_down, match_up, down_ref, up_ref, *outs):
    grouped_refs, pieces = outs[:2], outs[2:]
    write_normed(chips, x_ref, pieces)
    blocks, rows, inner = down_ref.shape
    unit = pieces[0].shape[-1]
    own = x_ref.shape[1] // chips // unit
    for leg, (match, ref) in enumerate(((match_down, down_ref), (match_up, up_ref))):
        for m in range(blocks):
            chosen = ref[0].astype(jnp.float32)
            for j in range(1, blocks):
                mine = match[m, j : j + 1, 0:1] != 0
                chosen = jnp.where(mine, ref[j].astype(jnp.float32), chosen)
            chosen = chosen.astype(x_ref.dtype)
            grouped_refs[leg][m * rows : (m + 1) * rows, :] = chosen
            for piece in pieces:
                for b in range(inner // unit):
                    piece[own + leg * (inner // unit) + b, m * rows : (m + 1) * rows, :] = chosen[
                        :, b * unit : (b + 1) * unit
                    ]


def up_kernel(chips, x_ref, *pieces):
    write_normed(chips, x_ref, pieces)


def pieces_down(x, sums_down, sums_up, match_down, match_up, members):
    rows, width = x.shape
    inner = sums_down.shape[1]
    chips = members // 2
    unit = unit_of(width, members, inner)
    count = width // chips // unit + 2 * inner // unit
    blocks = match_down.shape[0]
    cut = (blocks, rows // blocks, inner)
    outputs = [jax.ShapeDtypeStruct((rows, inner), x.dtype)] * 2
    outputs += [jax.ShapeDtypeStruct((count, rows, unit), x.dtype)] * chips
    return called(
        functools.partial(down_kernel, chips),
        (x, match_down, match_up, sums_down.reshape(cut), sums_up.reshape(cut)),
        outputs,
        flops=4 * rows * width,
    )


def pieces_up(x, inner, members):
    rows, width = x.shape
    chips = members // 2
    unit = unit_of(width, members, inner)
    outputs = [jax.ShapeDtypeStruct((width // chips // unit, rows, unit), x.dtype)] * chips
    return called(functools.partial(up_kernel, chips), (x,), outputs, flops=4 * rows * width)


def product_kernel(chips, inner, *refs):
    down, up = refs[:chips], refs[chips : 2 * chips]
    keep_ref, send_ref = refs[2 * chips :]
    unit = down[0].shape[-1]
    half = keep_ref.shape[0] // unit
    own = 2 * half
    core = lax.axis_index("dp") % 2
    over_tokens = (((0,), (0,)), ((), ()))

    def stacked(at, grouped):
        legs = [ref[at[0]] for ref in down]
        legs += [ref[at[1]] for ref in (down if grouped else up)]
        return jnp.concatenate(legs, axis=0)

    for g in range(inner // unit):
        grouped = stacked((own + g, own + inner // unit + g), True)
        for dest, out_ref in ((core, keep_ref), (1 - core, send_ref)):
            for b in range(half):
                at = dest * half + b
                out_ref[b * unit : (b + 1) * unit, g * unit : (g + 1) * unit] = lax.dot_general(
                    stacked((at, at), False),
                    grouped,
                    over_tokens,
                    preferred_element_type=jnp.float32,
                )


def products(down, up, width, inner, members):
    chips = members // 2
    rows = up[0].shape[1]
    out = jax.ShapeDtypeStruct((width // members, inner), jnp.float32)
    return called(
        functools.partial(product_kernel, chips, inner),
        (*down, *up),
        [out, out],
        flops=8 * chips * rows * (width // members) * inner,
        vmem=8,
    )


def combine_kernel(factor, keep_ref, got_ref, out_ref, held, sent):
    slots, step, _ = held.shape
    copies = []
    for i in range(slots):
        at = i * step
        held[i] = (keep_ref[at : at + step, :] + got_ref[at : at + step, :]) * factor
        copies.append(
            pltpu.make_async_copy(held.at[i], out_ref.at[pl.ds(at, step), :], sent.at[i])
        )
        copies[-1].start()
    for copy in copies:
        copy.wait()


def combined(keep, got, factor):
    rows, inner = keep.shape
    slots = 4
    return pl.pallas_call(
        functools.partial(combine_kernel, factor),
        in_specs=[whole_vmem()] * 2,
        out_specs=pl.BlockSpec(memory_space=pltpu.HBM),
        out_shape=jax.ShapeDtypeStruct(keep.shape, keep.dtype),
        scratch_shapes=[
            pltpu.VMEM((slots, rows // slots, inner), keep.dtype),
            pltpu.SemaphoreType.DMA((slots,)),
        ],
        name="combine",
        compiler_params=pltpu.CompilerParams(vmem_limit_bytes=4 * MIB),
        cost_estimate=pl.CostEstimate(
            flops=2 * rows * inner, bytes_accessed=12 * rows * inner, transcendentals=0
        ),
    )(keep, got)


def weight_copies(weight_ref, held, arrived):
    tiles, tile, _ = held.shape
    copies = [
        pltpu.make_async_copy(weight_ref.at[pl.ds(t * tile, tile), :], held.at[t], arrived.at[t])
        for t in range(tiles)
    ]
    for copy in copies:
        copy.start()
    return copies


def write_span(x_ref, scaled, back, values, total, inverse, next_ref, through_ref):
    rows, width = x_ref.shape
    mean = jnp.sum(total, axis=-1, keepdims=True) * (1.0 / width)
    mean = jnp.broadcast_to(mean, (rows, HD))
    inverse = jnp.broadcast_to(inverse, (rows, HD))
    for k in range(KVH):
        spread = values[:, k * HD : (k + 1) * HD]
        for j in range(GROUPS):
            at = slice((k * GROUPS + j) * HD, (k * GROUPS + j + 1) * HD)
            next_ref[:, at] = (x_ref[:, at].astype(jnp.float32) + spread).astype(next_ref.dtype)
            through_ref[:, at] = inverse * (back[:, at] - scaled[:, at] * mean)


def early_kernel(
    x_ref, down_ref, up_ref, weight_ref,
    next_ref, through_ref, back_ref,
    scaled, back, held, arrived,
):
    rows, _ = x_ref.shape
    tile, inner = held.shape[1:]
    copies = weight_copies(weight_ref, held, arrived)
    x = x_ref[...].astype(jnp.float32)
    inverse = inverse_of(x)
    scaled[...] = x * inverse
    values = jnp.zeros((rows, inner), jnp.float32)
    total = jnp.zeros((rows, HD), jnp.float32)
    grouped = jnp.concatenate([down_ref[...], up_ref[...]], axis=0)
    for t, copy in enumerate(copies):
        copy.wait()
        weight = held[t]
        at = slice(t * tile, (t + 1) * tile)
        normed = scaled[:, at].astype(x_ref.dtype)
        values = values + jnp.dot(normed, weight, preferred_element_type=jnp.float32)
        part = lax.dot_general(
            grouped, weight, (((1,), (1,)), ((), ())), preferred_element_type=jnp.float32
        )
        back[:, at] = part[:rows]
        back_ref[:, at] = part[rows:]
        for c in range(tile // HD):
            lanes = slice(c * HD, (c + 1) * HD)
            both = slice(t * tile + c * HD, t * tile + (c + 1) * HD)
            total = total + part[:rows, lanes] * scaled[:, both]
    write_span(x_ref, scaled, back, values, total, inverse, next_ref, through_ref)


def late_kernel(x_ref, back_ref, weight_ref, next_ref, through_ref, scaled, held, arrived):
    rows, _ = x_ref.shape
    tile, inner = held.shape[1:]
    copies = weight_copies(weight_ref, held, arrived)
    x = x_ref[...].astype(jnp.float32)
    inverse = inverse_of(x)
    scaled[...] = x * inverse
    values = jnp.zeros((rows, inner), jnp.float32)
    total = jnp.zeros((rows, HD), jnp.float32)
    for t, copy in enumerate(copies):
        copy.wait()
        at = slice(t * tile, (t + 1) * tile)
        normed = scaled[:, at].astype(x_ref.dtype)
        values = values + jnp.dot(normed, held[t], preferred_element_type=jnp.float32)
        for c in range(tile // HD):
            both = slice(t * tile + c * HD, t * tile + (c + 1) * HD)
            total = total + back_ref[:, both] * scaled[:, both]
    write_span(x_ref, scaled, back_ref, values, total, inverse, next_ref, through_ref)


def span(kernel, operands, weight, outputs, held, passes):
    rows, width = operands[0].shape
    inner = weight.shape[1]
    tile = math.gcd(width, 512)
    wide = jax.ShapeDtypeStruct((rows, width), jnp.float32)
    return called(
        kernel,
        (*operands, pltpu.with_memory_space_constraint(weight, pltpu.HBM)),
        [jax.ShapeDtypeStruct((rows, width), operands[0].dtype)] + [wide] * outputs,
        scratch=[pltpu.VMEM((rows, width), jnp.float32)] * held
        + [
            pltpu.VMEM((width // tile, tile, inner), weight.dtype),
            pltpu.SemaphoreType.DMA((width // tile,)),
        ],
        flops=2 * passes * rows * width * inner,
        vmem=10,
        in_specs=[whole_vmem()] * len(operands) + [pl.BlockSpec(memory_space=pltpu.HBM)],
    )


def finish_kernel(parts, match_ref, through_ref, *refs):
    raw = refs[0]
    out_ref, held, sent = refs[-3:]
    blocks = raw.shape[0]
    half = raw.shape[1] // len(parts)
    copies = []
    for i, part in enumerate(parts):
        inside = slice(i * half, (i + 1) * half)
        for m in range(blocks):
            chosen = raw[0, inside, :].astype(jnp.float32)
            for j in range(1, blocks):
                mine = match_ref[m, j : j + 1, 0:1] != 0
                chosen = jnp.where(mine, raw[j, inside, :].astype(jnp.float32), chosen)
            at = (2 * m + part) * half
            slot = i * blocks + m
            held[slot] = (chosen + through_ref[at : at + half, :]).astype(held.dtype)
            copies.append(
                pltpu.make_async_copy(
                    held.at[slot], out_ref.at[pl.ds(at, half), :], sent.at[slot]
                )
            )
            copies[-1].start()
    for copy in copies:
        copy.wait()


def finished(raw, parts, match, through, before=None):
    rows, width = through.shape
    blocks = raw.shape[0]
    half = raw.shape[1] // len(parts)
    slots = blocks * len(parts)
    operands = [match, through, raw] + ([] if before is None else [before])
    specs = [whole_vmem()] * 3
    if before is not None:
        specs.append(pl.BlockSpec(memory_space=pltpu.HBM))
    return pl.pallas_call(
        functools.partial(finish_kernel, parts),
        in_specs=specs,
        out_specs=pl.BlockSpec(memory_space=pltpu.HBM),
        out_shape=jax.ShapeDtypeStruct((rows, width), raw.dtype),
        scratch_shapes=[
            pltpu.VMEM((slots, half, width), raw.dtype),
            pltpu.SemaphoreType.DMA((slots,)),
        ],
        input_output_aliases={} if before is None else {len(operands) - 1: 0},
        name="finished",
        compiler_params=pltpu.CompilerParams(vmem_limit_bytes=4 * MIB),
        cost_estimate=pl.CostEstimate(
            flops=2 * slots * half * width,
            bytes_accessed=8 * slots * half * width,
            transcendentals=0,
        ),
    )(*operands)


def matches(roster_row):
    blocks = roster_row.shape[0]
    wanted = jnp.arange(blocks, dtype=jnp.int32)
    equal = (roster_row[None, :] == wanted[:, None]).astype(jnp.int32)
    return jnp.broadcast_to(equal[:, :, None], (blocks, blocks, HD))


def on_device(feed_down, feed_up, cotangent_down, cotangent_up, roster, value_weight):
    members = lax.axis_size("dp")
    chips = members // 2
    weight = value_weight[0]
    rows, width = feed_down.shape[1:]
    inner = weight.shape[1]
    match_down = matches(roster[0, 0])
    match_up = matches(roster[0, 1])

    sums_down, sums_up, *halves = group_sums(
        cotangent_down[0], cotangent_up[0], roster.shape[2]
    )
    x_down = passed_along(feed_down[0], "section", 1)
    sums_up = passed_along(sums_up, "section", 1)
    sums_down = passed_along(sums_down, "section", -1)
    x_up = passed_along(feed_up[0], "section", -1)
    raw_up = [passed_along(half, "section", 1) for half in halves]
    raw_down = passed_along(cotangent_down[0], "section", -1)

    def exchanged(pieces):
        got = [pieces[0]]
        for c in range(1, chips):
            to = [(i, ((i // 2) ^ c) * 2 + i % 2) for i in range(members)]
            got.append(lax.ppermute(pieces[c], "dp", to))
        return got

    grouped_down, grouped_up, *sent_down = pieces_down(x_down, sums_down, sums_up, match_down, match_up, members)
    got_down = exchanged(sent_down)
    got_up = exchanged(pieces_up(x_up, inner, members))

    next_down, through_down, back_norm = span(
        early_kernel, (x_down, grouped_down, grouped_up), weight, 2, 2, 3
    )
    next_up, through_up = span(late_kernel, (x_up, back_norm), weight, 1, 1, 1)

    keep, send = products(got_down, got_up, width, inner, members)
    got = lax.ppermute(send, "dp", [(i, i ^ 1) for i in range(members)])
    summed = combined(keep, got, float(2 * rows * members) ** (-0.5))

    blocks = roster.shape[2]
    raw_down = raw_down.reshape(blocks, rows // blocks, width)
    back_down = finished(raw_down, (0, 1), match_down, through_down)
    part_up = finished(raw_up[0], (0,), match_up, through_up)
    back_up = finished(raw_up[1], (1,), match_up, through_up, before=part_up)
    return (
        next_down[None],
        next_up[None],
        back_down[None],
        back_up[None],
        summed[None],
    )


def solution(mesh):
    rows = P("section", "dp", None)
    kept = P("section", None, None)
    return jax.shard_map(
        on_device,
        mesh=mesh,
        in_specs=(rows, rows, rows, rows, kept, kept),
        out_specs=(rows, rows, rows, rows, rows),
        check_vma=False,
    )
```

```python
import functools
import math

import jax
import jax.numpy as jnp
from jax import lax
from jax.experimental import pallas as pl
from jax.experimental.pallas import tpu as pltpu
from jax.sharding import PartitionSpec as P


KVH = 4
HD = 128
GROUPS = 8


EPSILON = 1e-05


MIB = 2**20


def passed_along(shard, axis, by):
    count = lax.axis_size(axis)
    return lax.ppermute(shard, axis, [(i, (i + by) % count) for i in range(count)])


def whole_vmem():
    return pl.BlockSpec(memory_space=pltpu.VMEM)


def called(kernel, operands, outputs, scratch=(), flops=0, vmem=4, **more):
    moved = sum(x.size * x.dtype.itemsize for x in list(operands) + list(outputs))
    return pl.pallas_call(
        kernel,
        in_specs=more.get("in_specs", [whole_vmem()] * len(operands)),
        out_specs=[whole_vmem()] * len(outputs),
        out_shape=list(outputs),
        scratch_shapes=list(scratch),
        compiler_params=pltpu.CompilerParams(vmem_limit_bytes=vmem * MIB),
        cost_estimate=pl.CostEstimate(
            flops=flops, bytes_accessed=moved, transcendentals=0
        ),
    )(*operands)


def group_kernel(early_ref, late_ref, early_out, late_out, *halves):
    part = pl.program_id(1)
    for src, dst in ((early_ref, early_out), (late_ref, late_out)):
        for k in range(KVH):
            total = src[:, k * GROUPS * HD : (k * GROUPS + 1) * HD].astype(jnp.float32)
            for j in range(1, GROUPS):
                at = (k * GROUPS + j) * HD
                total = total + src[:, at : at + HD].astype(jnp.float32)
            dst[:, k * HD : (k + 1) * HD] = total.astype(dst.dtype)

    for own in range(2):

        @pl.when(part == own)
        def _():
            halves[own][0] = late_ref[...]


def group_sums(early, late, blocks):
    rows, width = early.shape
    step = rows // blocks // 2
    wide = pl.BlockSpec((step, width), lambda j, i: (2 * j + i, 0))
    narrow = pl.BlockSpec((step, width // GROUPS), lambda j, i: (2 * j + i, 0))
    half = pl.BlockSpec((1, step, width), lambda j, i: (j, 0, 0))
    out = jax.ShapeDtypeStruct((rows, width // GROUPS), early.dtype)
    return pl.pallas_call(
        group_kernel,
        grid=(blocks, 2),
        in_specs=[wide, wide],
        out_specs=[narrow, narrow] + [half] * 2,
        out_shape=[out, out] + [jax.ShapeDtypeStruct((blocks, step, width), early.dtype)] * 2,
        name="group_sums",
        compiler_params=pltpu.CompilerParams(vmem_limit_bytes=6 * MIB),
        cost_estimate=pl.CostEstimate(
            flops=2 * rows * width, bytes_accessed=6 * rows * width, transcendentals=0
        ),
    )(early, late)


def inverse_of(x):
    return lax.rsqrt(jnp.mean(x * x, axis=-1, keepdims=True) + EPSILON)


def unit_of(width, members, inner):
    return math.gcd(width // members, inner)


def write_normed(chips, x_ref, piece_refs):
    inverse = inverse_of(x_ref[...].astype(jnp.float32))
    unit = piece_refs[0].shape[-1]
    per_chip = x_ref.shape[1] // chips
    chip = lax.axis_index("dp") // 2
    for c, piece in enumerate(piece_refs):
        base = (chip ^ c) * per_chip
        for b in range(per_chip // unit):
            at = pl.ds(pl.multiple_of(base + b * unit, unit), unit)
            piece[b] = (x_ref[:, at].astype(jnp.float32) * inverse).astype(piece.dtype)


def early_pieces_kernel(chips, x_ref, match_early, match_late, early_ref, late_ref, *outs):
    grouped_refs, pieces = outs[:2], outs[2:]
    write_normed(chips, x_ref, pieces)
    blocks, rows, inner = early_ref.shape
    unit = pieces[0].shape[-1]
    own = x_ref.shape[1] // chips // unit
    for leg, (match, ref) in enumerate(((match_early, early_ref), (match_late, late_ref))):
        for m in range(blocks):
            chosen = ref[0].astype(jnp.float32)
            for j in range(1, blocks):
                mine = match[m, j : j + 1, 0:1] != 0
                chosen = jnp.where(mine, ref[j].astype(jnp.float32), chosen)
            chosen = chosen.astype(x_ref.dtype)
            grouped_refs[leg][m * rows : (m + 1) * rows, :] = chosen
            for piece in pieces:
                for b in range(inner // unit):
                    piece[own + leg * (inner // unit) + b, m * rows : (m + 1) * rows, :] = chosen[
                        :, b * unit : (b + 1) * unit
                    ]


def late_pieces_kernel(chips, x_ref, *pieces):
    write_normed(chips, x_ref, pieces)


def pieces_early(x, sums_early, sums_late, match_early, match_late, members):
    rows, width = x.shape
    inner = sums_early.shape[1]
    chips = members // 2
    unit = unit_of(width, members, inner)
    count = width // chips // unit + 2 * inner // unit
    blocks = match_early.shape[0]
    cut = (blocks, rows // blocks, inner)
    outputs = [jax.ShapeDtypeStruct((rows, inner), x.dtype)] * 2
    outputs += [jax.ShapeDtypeStruct((count, rows, unit), x.dtype)] * chips
    return called(
        functools.partial(early_pieces_kernel, chips),
        (x, match_early, match_late, sums_early.reshape(cut), sums_late.reshape(cut)),
        outputs,
        flops=4 * rows * width,
    )


def pieces_late(x, inner, members):
    rows, width = x.shape
    chips = members // 2
    unit = unit_of(width, members, inner)
    outputs = [jax.ShapeDtypeStruct((width // chips // unit, rows, unit), x.dtype)] * chips
    return called(
        functools.partial(late_pieces_kernel, chips), (x,), outputs, flops=4 * rows * width
    )


def product_kernel(chips, inner, *refs):
    early, late = refs[:chips], refs[chips : 2 * chips]
    keep_ref, send_ref = refs[2 * chips :]
    unit = early[0].shape[-1]
    half = keep_ref.shape[0] // unit
    own = 2 * half
    core = lax.axis_index("dp") % 2
    over_tokens = (((0,), (0,)), ((), ()))

    def stacked(at, grouped):
        legs = [ref[at[0]] for ref in early]
        legs += [ref[at[1]] for ref in (early if grouped else late)]
        return jnp.concatenate(legs, axis=0)

    for g in range(inner // unit):
        grouped = stacked((own + g, own + inner // unit + g), True)
        for dest, out_ref in ((core, keep_ref), (1 - core, send_ref)):
            for b in range(half):
                at = dest * half + b
                out_ref[b * unit : (b + 1) * unit, g * unit : (g + 1) * unit] = lax.dot_general(
                    stacked((at, at), False),
                    grouped,
                    over_tokens,
                    preferred_element_type=jnp.float32,
                )


def products(early, late, width, inner, members):
    chips = members // 2
    rows = late[0].shape[1]
    out = jax.ShapeDtypeStruct((width // members, inner), jnp.float32)
    return called(
        functools.partial(product_kernel, chips, inner),
        (*early, *late),
        [out, out],
        flops=8 * chips * rows * (width // members) * inner,
        vmem=8,
    )


def combine_kernel(factor, keep_ref, got_ref, out_ref, held, sent):
    slots, step, _ = held.shape
    copies = []
    for i in range(slots):
        at = i * step
        held[i] = (keep_ref[at : at + step, :] + got_ref[at : at + step, :]) * factor
        copies.append(
            pltpu.make_async_copy(held.at[i], out_ref.at[pl.ds(at, step), :], sent.at[i])
        )
        copies[-1].start()
    for copy in copies:
        copy.wait()


def combined(keep, got, factor):
    rows, inner = keep.shape
    slots = 4
    return pl.pallas_call(
        functools.partial(combine_kernel, factor),
        in_specs=[whole_vmem()] * 2,
        out_specs=pl.BlockSpec(memory_space=pltpu.HBM),
        out_shape=jax.ShapeDtypeStruct(keep.shape, keep.dtype),
        scratch_shapes=[
            pltpu.VMEM((slots, rows // slots, inner), keep.dtype),
            pltpu.SemaphoreType.DMA((slots,)),
        ],
        name="combine",
        compiler_params=pltpu.CompilerParams(vmem_limit_bytes=4 * MIB),
        cost_estimate=pl.CostEstimate(
            flops=2 * rows * inner, bytes_accessed=12 * rows * inner, transcendentals=0
        ),
    )(keep, got)


def weight_copies(weight_ref, held, arrived):
    tiles, tile, _ = held.shape
    copies = [
        pltpu.make_async_copy(weight_ref.at[pl.ds(t * tile, tile), :], held.at[t], arrived.at[t])
        for t in range(tiles)
    ]
    for copy in copies:
        copy.start()
    return copies


def write_span(x_ref, scaled, back, values, total, inverse, next_ref, through_ref):
    rows, width = x_ref.shape
    mean = jnp.sum(total, axis=-1, keepdims=True) * (1.0 / width)
    mean = jnp.broadcast_to(mean, (rows, HD))
    inverse = jnp.broadcast_to(inverse, (rows, HD))
    for k in range(KVH):
        spread = values[:, k * HD : (k + 1) * HD]
        for j in range(GROUPS):
            at = slice((k * GROUPS + j) * HD, (k * GROUPS + j + 1) * HD)
            next_ref[:, at] = (x_ref[:, at].astype(jnp.float32) + spread).astype(next_ref.dtype)
            through_ref[:, at] = inverse * (back[:, at] - scaled[:, at] * mean)


def first_span_kernel(
    x_ref, early_ref, late_ref, weight_ref,
    next_ref, through_ref, back_ref,
    scaled, back, held, arrived,
):
    rows, _ = x_ref.shape
    tile, inner = held.shape[1:]
    copies = weight_copies(weight_ref, held, arrived)
    x = x_ref[...].astype(jnp.float32)
    inverse = inverse_of(x)
    scaled[...] = x * inverse
    values = jnp.zeros((rows, inner), jnp.float32)
    total = jnp.zeros((rows, HD), jnp.float32)
    grouped = jnp.concatenate([early_ref[...], late_ref[...]], axis=0)
    for t, copy in enumerate(copies):
        copy.wait()
        weight = held[t]
        at = slice(t * tile, (t + 1) * tile)
        normed = scaled[:, at].astype(x_ref.dtype)
        values = values + jnp.dot(normed, weight, preferred_element_type=jnp.float32)
        part = lax.dot_general(
            grouped, weight, (((1,), (1,)), ((), ())), preferred_element_type=jnp.float32
        )
        back[:, at] = part[:rows]
        back_ref[:, at] = part[rows:]
        for c in range(tile // HD):
            lanes = slice(c * HD, (c + 1) * HD)
            both = slice(t * tile + c * HD, t * tile + (c + 1) * HD)
            total = total + part[:rows, lanes] * scaled[:, both]
    write_span(x_ref, scaled, back, values, total, inverse, next_ref, through_ref)


def second_span_kernel(x_ref, back_ref, weight_ref, next_ref, through_ref, scaled, held, arrived):
    rows, _ = x_ref.shape
    tile, inner = held.shape[1:]
    copies = weight_copies(weight_ref, held, arrived)
    x = x_ref[...].astype(jnp.float32)
    inverse = inverse_of(x)
    scaled[...] = x * inverse
    values = jnp.zeros((rows, inner), jnp.float32)
    total = jnp.zeros((rows, HD), jnp.float32)
    for t, copy in enumerate(copies):
        copy.wait()
        at = slice(t * tile, (t + 1) * tile)
        normed = scaled[:, at].astype(x_ref.dtype)
        values = values + jnp.dot(normed, held[t], preferred_element_type=jnp.float32)
        for c in range(tile // HD):
            both = slice(t * tile + c * HD, t * tile + (c + 1) * HD)
            total = total + back_ref[:, both] * scaled[:, both]
    write_span(x_ref, scaled, back_ref, values, total, inverse, next_ref, through_ref)


def span(kernel, operands, weight, outputs, held, passes):
    rows, width = operands[0].shape
    inner = weight.shape[1]
    tile = math.gcd(width, 512)
    wide = jax.ShapeDtypeStruct((rows, width), jnp.float32)
    return called(
        kernel,
        (*operands, pltpu.with_memory_space_constraint(weight, pltpu.HBM)),
        [jax.ShapeDtypeStruct((rows, width), operands[0].dtype)] + [wide] * outputs,
        scratch=[pltpu.VMEM((rows, width), jnp.float32)] * held
        + [
            pltpu.VMEM((width // tile, tile, inner), weight.dtype),
            pltpu.SemaphoreType.DMA((width // tile,)),
        ],
        flops=2 * passes * rows * width * inner,
        vmem=10,
        in_specs=[whole_vmem()] * len(operands) + [pl.BlockSpec(memory_space=pltpu.HBM)],
    )


def finish_kernel(parts, match_ref, through_ref, *refs):
    raw = refs[0]
    out_ref, held, sent = refs[-3:]
    blocks = raw.shape[0]
    half = raw.shape[1] // len(parts)
    copies = []
    for i, part in enumerate(parts):
        inside = slice(i * half, (i + 1) * half)
        for m in range(blocks):
            chosen = raw[0, inside, :].astype(jnp.float32)
            for j in range(1, blocks):
                mine = match_ref[m, j : j + 1, 0:1] != 0
                chosen = jnp.where(mine, raw[j, inside, :].astype(jnp.float32), chosen)
            at = (2 * m + part) * half
            slot = i * blocks + m
            held[slot] = (chosen + through_ref[at : at + half, :]).astype(held.dtype)
            copies.append(
                pltpu.make_async_copy(
                    held.at[slot], out_ref.at[pl.ds(at, half), :], sent.at[slot]
                )
            )
            copies[-1].start()
    for copy in copies:
        copy.wait()


def finished(raw, parts, match, through, before=None):
    rows, width = through.shape
    blocks = raw.shape[0]
    half = raw.shape[1] // len(parts)
    slots = blocks * len(parts)
    operands = [match, through, raw] + ([] if before is None else [before])
    specs = [whole_vmem()] * 3
    if before is not None:
        specs.append(pl.BlockSpec(memory_space=pltpu.HBM))
    return pl.pallas_call(
        functools.partial(finish_kernel, parts),
        in_specs=specs,
        out_specs=pl.BlockSpec(memory_space=pltpu.HBM),
        out_shape=jax.ShapeDtypeStruct((rows, width), raw.dtype),
        scratch_shapes=[
            pltpu.VMEM((slots, half, width), raw.dtype),
            pltpu.SemaphoreType.DMA((slots,)),
        ],
        input_output_aliases={} if before is None else {len(operands) - 1: 0},
        name="finished",
        compiler_params=pltpu.CompilerParams(vmem_limit_bytes=4 * MIB),
        cost_estimate=pl.CostEstimate(
            flops=2 * slots * half * width,
            bytes_accessed=8 * slots * half * width,
            transcendentals=0,
        ),
    )(*operands)


def matches(roster_row):
    blocks = roster_row.shape[0]
    wanted = jnp.arange(blocks, dtype=jnp.int32)
    equal = (roster_row[None, :] == wanted[:, None]).astype(jnp.int32)
    return jnp.broadcast_to(equal[:, :, None], (blocks, blocks, HD))


def relayed(
    feed_early, feed_late, cotangent_early, cotangent_late, roster_early, roster_late, weight, by
):
    members = lax.axis_size("dp")
    chips = members // 2
    rows, width = feed_early.shape
    inner = weight.shape[1]
    match_early = matches(roster_early)
    match_late = matches(roster_late)

    sums_early, sums_late, *halves = group_sums(
        cotangent_early, cotangent_late, roster_early.shape[0]
    )
    x_early = passed_along(feed_early, "section", by)
    sums_late = passed_along(sums_late, "section", by)
    sums_early = passed_along(sums_early, "section", -by)
    x_late = passed_along(feed_late, "section", -by)
    raw_late = [passed_along(half, "section", by) for half in halves]
    raw_early = passed_along(cotangent_early, "section", -by)

    def exchanged(pieces):
        got = [pieces[0]]
        for c in range(1, chips):
            to = [(i, ((i // 2) ^ c) * 2 + i % 2) for i in range(members)]
            got.append(lax.ppermute(pieces[c], "dp", to))
        return got

    grouped_early, grouped_late, *sent_early = pieces_early(x_early, sums_early, sums_late, match_early, match_late, members)
    got_early = exchanged(sent_early)
    got_late = exchanged(pieces_late(x_late, inner, members))

    next_early, through_early, back_norm = span(
        first_span_kernel, (x_early, grouped_early, grouped_late), weight, 2, 2, 3
    )
    next_late, through_late = span(second_span_kernel, (x_late, back_norm), weight, 1, 1, 1)

    keep, send = products(got_early, got_late, width, inner, members)
    got = lax.ppermute(send, "dp", [(i, i ^ 1) for i in range(members)])
    summed = combined(keep, got, float(2 * rows * members) ** (-0.5))

    blocks = roster_early.shape[0]
    raw_early = raw_early.reshape(blocks, rows // blocks, width)
    back_early = finished(raw_early, (0, 1), match_early, through_early)
    part_late = finished(raw_late[0], (0,), match_late, through_late)
    back_late = finished(raw_late[1], (1,), match_late, through_late, before=part_late)
    return next_early, next_late, back_early, back_late, summed


def on_device(feed_down, feed_up, cotangent_down, cotangent_up, roster, value_weight):
    next_up, next_down, back_up, back_down, summed = relayed(
        feed_up[0],
        feed_down[0],
        cotangent_up[0],
        cotangent_down[0],
        roster[0, 1],
        roster[0, 0],
        value_weight[0],
        -1,
    )
    return (
        next_down[None],
        next_up[None],
        back_down[None],
        back_up[None],
        summed[None],
    )


def solution(mesh):
    rows = P("section", "dp", None)
    kept = P("section", None, None)
    return jax.shard_map(
        on_device,
        mesh=mesh,
        in_specs=(rows, rows, rows, rows, kept, kept),
        out_specs=(rows, rows, rows, rows, rows),
        check_vma=False,
    )
```

```python
import functools
import math

import jax
import jax.numpy as jnp
from jax import lax
from jax.experimental import pallas as pl
from jax.experimental.pallas import tpu as pltpu
from jax.sharding import PartitionSpec as P


KVH = 4
HD = 128
GROUPS = 8


EPSILON = 1e-05


MIB = 2**20


def passed_along(shard, axis, by):
    count = lax.axis_size(axis)
    return lax.ppermute(shard, axis, [(i, (i + by) % count) for i in range(count)])


def whole_vmem():
    return pl.BlockSpec(memory_space=pltpu.VMEM)


def called(kernel, operands, outputs, scratch=(), flops=0, vmem=4, **more):
    moved = sum(x.size * x.dtype.itemsize for x in list(operands) + list(outputs))
    return pl.pallas_call(
        kernel,
        in_specs=more.get("in_specs", [whole_vmem()] * len(operands)),
        out_specs=[whole_vmem()] * len(outputs),
        out_shape=list(outputs),
        scratch_shapes=list(scratch),
        compiler_params=pltpu.CompilerParams(vmem_limit_bytes=vmem * MIB),
        cost_estimate=pl.CostEstimate(
            flops=flops, bytes_accessed=moved, transcendentals=0
        ),
    )(*operands)


def group_sum(load):
    sums = []
    for k in range(KVH):
        total = load(k * GROUPS * HD).astype(jnp.float32)
        for j in range(1, GROUPS):
            total = total + load((k * GROUPS + j) * HD).astype(jnp.float32)
        sums.append(total)
    return sums


def group_kernel(
    early_ref, late_ref, early_out, late_out, first_out, rest_out, second_out
):
    block = pl.program_id(0)
    part = pl.program_id(1)
    opening = (part == 0) & (block == 0)
    for k, total in enumerate(group_sum(lambda at: early_ref[:, at : at + HD])):
        early_out[:, k * HD : (k + 1) * HD] = total.astype(early_out.dtype)

    @pl.when(opening)
    def _():
        first_out[0] = late_ref[...]

    @pl.when(jnp.logical_not(opening))
    def _():
        for k, total in enumerate(group_sum(lambda at: late_ref[:, at : at + HD])):
            late_out[0, :, k * HD : (k + 1) * HD] = total.astype(late_out.dtype)

    @pl.when((part == 0) & (block > 0))
    def _():
        rest_out[0] = late_ref[...]

    @pl.when(part == 1)
    def _():
        second_out[0] = late_ref[...]


def group_sums(early, late, blocks):
    rows, width = early.shape
    inner = width // GROUPS
    step = rows // blocks // 2
    wide = pl.BlockSpec((step, width), lambda j, i: (2 * j + i, 0))
    narrow = pl.BlockSpec((step, inner), lambda j, i: (2 * j + i, 0))
    later = pl.BlockSpec((1, step, inner), lambda j, i: (jnp.maximum(2 * j + i - 1, 0), 0, 0))
    shape = (1, step, width)
    first = pl.BlockSpec(shape, lambda j, i: (0, 0, 0))
    rest = pl.BlockSpec(shape, lambda j, i: (jnp.maximum(j - 1, 0), 0, 0))
    second = pl.BlockSpec(shape, lambda j, i: (j, 0, 0))
    return pl.pallas_call(
        group_kernel,
        grid=(blocks, 2),
        in_specs=[wide, wide],
        out_specs=[narrow, later, first, rest, second],
        out_shape=[
            jax.ShapeDtypeStruct((rows, inner), early.dtype),
            jax.ShapeDtypeStruct((2 * blocks - 1, step, inner), late.dtype),
        ]
        + [
            jax.ShapeDtypeStruct((count, step, width), late.dtype)
            for count in (1, blocks - 1, blocks)
        ],
        name="group_sums",
        compiler_params=pltpu.CompilerParams(vmem_limit_bytes=6 * MIB),
        cost_estimate=pl.CostEstimate(
            flops=2 * rows * width, bytes_accessed=6 * rows * width, transcendentals=0
        ),
    )(early, late)


def inverse_of(x):
    return lax.rsqrt(jnp.mean(x * x, axis=-1, keepdims=True) + EPSILON)


def unit_of(width, members, inner):
    return math.gcd(width // members, inner)


def write_normed(chips, x_ref, piece_refs):
    inverse = inverse_of(x_ref[...].astype(jnp.float32))
    unit = piece_refs[0].shape[-1]
    per_chip = x_ref.shape[1] // chips
    chip = lax.axis_index("dp") // 2
    for c, piece in enumerate(piece_refs):
        base = (chip ^ c) * per_chip
        for b in range(per_chip // unit):
            at = pl.ds(pl.multiple_of(base + b * unit, unit), unit)
            piece[b] = (x_ref[:, at].astype(jnp.float32) * inverse).astype(piece.dtype)


def arranged(match_ref, m, block_of, blocks):
    chosen = block_of(0).astype(jnp.float32)
    for j in range(1, blocks):
        mine = match_ref[m, j : j + 1, 0:1] != 0
        chosen = jnp.where(mine, block_of(j).astype(jnp.float32), chosen)
    return chosen


def write_grouped(at, value, own, grouped_ref, piece_refs):
    rows, inner = value.shape
    unit = piece_refs[0].shape[-1]
    grouped_ref[at : at + rows, :] = value
    for piece in piece_refs:
        for b in range(inner // unit):
            piece[own + b, at : at + rows, :] = value[:, b * unit : (b + 1) * unit]


def early_pieces_kernel(chips, x_ref, match_ref, sums_ref, grouped_ref, *pieces):
    write_normed(chips, x_ref, pieces)
    blocks, rows, _ = sums_ref.shape
    own = x_ref.shape[1] // chips // pieces[0].shape[-1]
    for m in range(blocks):
        value = arranged(match_ref, m, lambda j: sums_ref[j], blocks).astype(x_ref.dtype)
        write_grouped(m * rows, value, own, grouped_ref, pieces)


def late_pieces_kernel(chips, x_ref, match_ref, first_ref, sums_ref, grouped_ref, *pieces):
    write_normed(chips, x_ref, pieces)
    half = first_ref.shape[1]
    blocks = match_ref.shape[0]
    own = x_ref.shape[1] // chips // pieces[0].shape[-1]
    first = group_sum(lambda at: first_ref[0, :, at : at + HD])
    first = jnp.concatenate(first, axis=-1).astype(x_ref.dtype)

    def sums_of(at):
        return first if at == 0 else sums_ref[at - 1]

    for part in range(2):
        for m in range(blocks):
            value = arranged(match_ref, m, lambda j: sums_of(2 * j + part), blocks)
            at = (2 * m + part) * half
            write_grouped(at, value.astype(x_ref.dtype), own, grouped_ref, pieces)


def pieces_of(kernel, x, operands, inner, members):
    rows, width = x.shape
    chips = members // 2
    unit = unit_of(width, members, inner)
    count = width // chips // unit + inner // unit
    outputs = [jax.ShapeDtypeStruct((rows, inner), x.dtype)]
    outputs += [jax.ShapeDtypeStruct((count, rows, unit), x.dtype)] * chips
    return called(functools.partial(kernel, chips), (x, *operands), outputs, flops=4 * rows * width)


def product_kernel(chips, inner, *refs):
    early, late = refs[:chips], refs[chips : 2 * chips]
    keep_ref, send_ref = refs[2 * chips :]
    unit = early[0].shape[-1]
    half = keep_ref.shape[0] // unit
    own = 2 * half
    core = lax.axis_index("dp") % 2
    over_tokens = (((0,), (0,)), ((), ()))

    def stacked(at):
        return jnp.concatenate([ref[at] for ref in (*early, *late)], axis=0)

    for g in range(inner // unit):
        grouped = stacked(own + g)
        for dest, out_ref in ((core, keep_ref), (1 - core, send_ref)):
            for b in range(half):
                out_ref[b * unit : (b + 1) * unit, g * unit : (g + 1) * unit] = lax.dot_general(
                    stacked(dest * half + b),
                    grouped,
                    over_tokens,
                    preferred_element_type=jnp.float32,
                )


def products(early, late, width, inner, members):
    chips = members // 2
    rows = late[0].shape[1]
    out = jax.ShapeDtypeStruct((width // members, inner), jnp.float32)
    return called(
        functools.partial(product_kernel, chips, inner),
        (*early, *late),
        [out, out],
        flops=8 * chips * rows * (width // members) * inner,
        vmem=8,
    )


def combine_kernel(factor, keep_ref, got_ref, out_ref, held, sent):
    slots, step, _ = held.shape
    copies = []
    for i in range(slots):
        at = i * step
        held[i] = (keep_ref[at : at + step, :] + got_ref[at : at + step, :]) * factor
        copies.append(
            pltpu.make_async_copy(held.at[i], out_ref.at[pl.ds(at, step), :], sent.at[i])
        )
        copies[-1].start()
    for copy in copies:
        copy.wait()


def combined(keep, got, factor):
    rows, inner = keep.shape
    slots = 4
    return pl.pallas_call(
        functools.partial(combine_kernel, factor),
        in_specs=[whole_vmem()] * 2,
        out_specs=pl.BlockSpec(memory_space=pltpu.HBM),
        out_shape=jax.ShapeDtypeStruct(keep.shape, keep.dtype),
        scratch_shapes=[
            pltpu.VMEM((slots, rows // slots, inner), keep.dtype),
            pltpu.SemaphoreType.DMA((slots,)),
        ],
        name="combine",
        compiler_params=pltpu.CompilerParams(vmem_limit_bytes=4 * MIB),
        cost_estimate=pl.CostEstimate(
            flops=2 * rows * inner, bytes_accessed=12 * rows * inner, transcendentals=0
        ),
    )(keep, got)


def span_kernel(x_ref, grouped_ref, weight_ref, next_ref, through_ref, scaled, back, held, arrived):
    rows, width = x_ref.shape
    tiles, tile, inner = held.shape
    copies = [
        pltpu.make_async_copy(weight_ref.at[pl.ds(t * tile, tile), :], held.at[t], arrived.at[t])
        for t in range(tiles)
    ]
    for copy in copies:
        copy.start()
    x = x_ref[...].astype(jnp.float32)
    inverse = inverse_of(x)
    scaled[...] = x * inverse
    values = jnp.zeros((rows, inner), jnp.float32)
    total = jnp.zeros((rows, HD), jnp.float32)
    grouped = grouped_ref[...]
    for t, copy in enumerate(copies):
        copy.wait()
        weight = held[t]
        at = slice(t * tile, (t + 1) * tile)
        normed = scaled[:, at].astype(x_ref.dtype)
        values = values + jnp.dot(normed, weight, preferred_element_type=jnp.float32)
        part = lax.dot_general(
            grouped, weight, (((1,), (1,)), ((), ())), preferred_element_type=jnp.float32
        )
        back[:, at] = part
        for c in range(tile // HD):
            lanes = slice(c * HD, (c + 1) * HD)
            total = total + part[:, lanes] * scaled[:, t * tile + c * HD : t * tile + (c + 1) * HD]
    mean = jnp.sum(total, axis=-1, keepdims=True) * (1.0 / width)
    mean = jnp.broadcast_to(mean, (rows, HD))
    inverse = jnp.broadcast_to(inverse, (rows, HD))
    for k in range(KVH):
        spread = values[:, k * HD : (k + 1) * HD]
        for j in range(GROUPS):
            at = slice((k * GROUPS + j) * HD, (k * GROUPS + j + 1) * HD)
            next_ref[:, at] = (x_ref[:, at].astype(jnp.float32) + spread).astype(next_ref.dtype)
            through_ref[:, at] = inverse * (back[:, at] - scaled[:, at] * mean)


def span(x, grouped, weight):
    rows, width = x.shape
    inner = weight.shape[1]
    tile = math.gcd(width, 512)
    return called(
        span_kernel,
        (x, grouped, pltpu.with_memory_space_constraint(weight, pltpu.HBM)),
        [
            jax.ShapeDtypeStruct((rows, width), x.dtype),
            jax.ShapeDtypeStruct((rows, width), jnp.float32),
        ],
        scratch=[
            pltpu.VMEM((rows, width), jnp.float32),
            pltpu.VMEM((rows, width), jnp.float32),
            pltpu.VMEM((width // tile, tile, inner), weight.dtype),
            pltpu.SemaphoreType.DMA((width // tile,)),
        ],
        flops=4 * rows * width * inner,
        vmem=10,
        in_specs=[whole_vmem()] * 2 + [pl.BlockSpec(memory_space=pltpu.HBM)],
    )


def finish_kernel(parts, places, match_ref, through_ref, *refs):
    out_ref, held, sent = refs[-3:]
    blocks = match_ref.shape[0]
    half = held.shape[1]
    copies = []
    for i, part in enumerate(parts):

        def received(j):
            operand, at = places[i * blocks + j]
            return refs[operand][at].astype(jnp.float32)

        for m in range(blocks):
            chosen = received(0)
            for j in range(1, blocks):
                mine = match_ref[m, j : j + 1, 0:1] != 0
                chosen = jnp.where(mine, received(j), chosen)
            at = (2 * m + part) * half
            slot = i * blocks + m
            held[slot] = (chosen + through_ref[at : at + half, :]).astype(held.dtype)
            copies.append(
                pltpu.make_async_copy(
                    held.at[slot], out_ref.at[pl.ds(at, half), :], sent.at[slot]
                )
            )
            copies[-1].start()
    for copy in copies:
        copy.wait()


def finished(raws, parts, places, match, through, before=None):
    rows, width = through.shape
    blocks = match.shape[0]
    slots = blocks * len(parts)
    half = rows // blocks // 2
    operands = [match, through, *raws] + ([] if before is None else [before])
    specs = [whole_vmem()] * (2 + len(raws))
    if before is not None:
        specs.append(pl.BlockSpec(memory_space=pltpu.HBM))
    return pl.pallas_call(
        functools.partial(finish_kernel, parts, places),
        in_specs=specs,
        out_specs=pl.BlockSpec(memory_space=pltpu.HBM),
        out_shape=jax.ShapeDtypeStruct((rows, width), raws[0].dtype),
        scratch_shapes=[
            pltpu.VMEM((slots, half, width), raws[0].dtype),
            pltpu.SemaphoreType.DMA((slots,)),
        ],
        input_output_aliases={} if before is None else {len(operands) - 1: 0},
        name="finished",
        compiler_params=pltpu.CompilerParams(vmem_limit_bytes=4 * MIB),
        cost_estimate=pl.CostEstimate(
            flops=2 * slots * half * width,
            bytes_accessed=8 * slots * half * width,
            transcendentals=0,
        ),
    )(*operands)


def matches(roster_row):
    blocks = roster_row.shape[0]
    wanted = jnp.arange(blocks, dtype=jnp.int32)
    equal = (roster_row[None, :] == wanted[:, None]).astype(jnp.int32)
    return jnp.broadcast_to(equal[:, :, None], (blocks, blocks, HD))


def relayed(
    feed_early, feed_late, cotangent_early, cotangent_late, roster_early, roster_late, weight, by
):
    members = lax.axis_size("dp")
    chips = members // 2
    rows, width = feed_early.shape
    inner = weight.shape[1]
    match_early = matches(roster_early)
    match_late = matches(roster_late)

    sums_early, sums_late, *pieces = group_sums(
        cotangent_early, cotangent_late, roster_early.shape[0]
    )
    x_early = passed_along(feed_early, "section", by)
    sums_late = passed_along(sums_late, "section", by)
    sums_early = passed_along(sums_early, "section", -by)
    x_late = passed_along(feed_late, "section", -by)
    raw_late = [passed_along(piece, "section", by) for piece in pieces]
    raw_early = passed_along(cotangent_early, "section", -by)

    def exchanged(pieces):
        got = [pieces[0]]
        for c in range(1, chips):
            to = [(i, ((i // 2) ^ c) * 2 + i % 2) for i in range(members)]
            got.append(lax.ppermute(pieces[c], "dp", to))
        return got

    blocks = roster_early.shape[0]
    sums_early = sums_early.reshape(blocks, rows // blocks, inner)
    grouped_early, *sent_early = pieces_of(
        early_pieces_kernel, x_early, (match_early, sums_early), inner, members
    )
    got_early = exchanged(sent_early)
    grouped_late, *sent_late = pieces_of(
        late_pieces_kernel, x_late, (match_late, raw_late[0], sums_late), inner, members
    )
    got_late = exchanged(sent_late)

    next_early, through_early = span(x_early, grouped_early, weight)
    next_late, through_late = span(x_late, grouped_late, weight)

    keep, send = products(got_early, got_late, width, inner, members)
    got = lax.ppermute(send, "dp", [(i, i ^ 1) for i in range(members)])
    summed = combined(keep, got, float(2 * rows * members) ** (-0.5))

    raw_early = [raw_early.reshape(2 * blocks, rows // blocks // 2, width)]
    whole = [(0, 2 * j + part) for part in range(2) for j in range(blocks)]
    firsts = [(min(j, 1), max(j - 1, 0)) for j in range(blocks)]
    seconds = [(0, j) for j in range(blocks)]
    back_early = finished(raw_early, (0, 1), whole, match_early, through_early)
    part_late = finished(raw_late[:2], (0,), firsts, match_late, through_late)
    back_late = finished(raw_late[2:], (1,), seconds, match_late, through_late, part_late)
    return next_early, next_late, back_early, back_late, summed


def on_device(feed_down, feed_up, cotangent_down, cotangent_up, roster, value_weight):
    next_up, next_down, back_up, back_down, summed = relayed(
        feed_up[0],
        feed_down[0],
        cotangent_up[0],
        cotangent_down[0],
        roster[0, 1],
        roster[0, 0],
        value_weight[0],
        -1,
    )
    return (
        next_down[None],
        next_up[None],
        back_down[None],
        back_up[None],
        summed[None],
    )


def solution(mesh):
    rows = P("section", "dp", None)
    kept = P("section", None, None)
    return jax.shard_map(
        on_device,
        mesh=mesh,
        in_specs=(rows, rows, rows, rows, kept, kept),
        out_specs=(rows, rows, rows, rows, rows),
        check_vma=False,
    )
```

```python
import functools
import math

import jax
import jax.numpy as jnp
from jax import lax
from jax.experimental import pallas as pl
from jax.experimental.pallas import tpu as pltpu
from jax.sharding import PartitionSpec as P


KVH = 4
HD = 128
GROUPS = 8


EPSILON = 1e-05


MIB = 2**20


def passed_along(shard, axis, by):
    count = lax.axis_size(axis)
    return lax.ppermute(shard, axis, [(i, (i + by) % count) for i in range(count)])


def whole_vmem():
    return pl.BlockSpec(memory_space=pltpu.VMEM)


def called(kernel, operands, outputs, scratch=(), flops=0, vmem=4, **more):
    moved = sum(x.size * x.dtype.itemsize for x in list(operands) + list(outputs))
    return pl.pallas_call(
        kernel,
        in_specs=more.get("in_specs", [whole_vmem()] * len(operands)),
        out_specs=[whole_vmem()] * len(outputs),
        out_shape=list(outputs),
        scratch_shapes=list(scratch),
        compiler_params=pltpu.CompilerParams(vmem_limit_bytes=vmem * MIB),
        cost_estimate=pl.CostEstimate(
            flops=flops, bytes_accessed=moved, transcendentals=0
        ),
    )(*operands)


def group_sum(load):
    sums = []
    for k in range(KVH):
        total = load(k * GROUPS * HD).astype(jnp.float32)
        for j in range(1, GROUPS):
            total = total + load((k * GROUPS + j) * HD).astype(jnp.float32)
        sums.append(total)
    return sums


def group_kernel(
    early_ref, late_ref, early_out, late_out, first_out, rest_out, second_out
):
    block = pl.program_id(0)
    part = pl.program_id(1)
    for k, total in enumerate(group_sum(lambda at: early_ref[:, at : at + HD])):
        early_out[:, k * HD : (k + 1) * HD] = total.astype(early_out.dtype)

    @pl.when((part == 0) & (block == 0))
    def _():
        first_out[0] = late_ref[...]

    @pl.when((part == 0) & (block > 0))
    def _():
        rest_out[0] = late_ref[...]

    @pl.when(part == 1)
    def _():
        second_out[0] = late_ref[...]
        for k, total in enumerate(group_sum(lambda at: late_ref[:, at : at + HD])):
            late_out[0, :, k * HD : (k + 1) * HD] = total.astype(late_out.dtype)


def group_sums(early, late, blocks):
    rows, width = early.shape
    inner = width // GROUPS
    step = rows // blocks // 2
    wide = pl.BlockSpec((step, width), lambda j, i: (2 * j + i, 0))
    narrow = pl.BlockSpec((step, inner), lambda j, i: (2 * j + i, 0))
    later = pl.BlockSpec((1, step, inner), lambda j, i: (j, 0, 0))
    shape = (1, step, width)
    first = pl.BlockSpec(shape, lambda j, i: (0, 0, 0))
    rest = pl.BlockSpec(shape, lambda j, i: (jnp.maximum(j - 1, 0), 0, 0))
    second = pl.BlockSpec(shape, lambda j, i: (j, 0, 0))
    return pl.pallas_call(
        group_kernel,
        grid=(blocks, 2),
        in_specs=[wide, wide],
        out_specs=[narrow, later, first, rest, second],
        out_shape=[
            jax.ShapeDtypeStruct((rows, inner), early.dtype),
            jax.ShapeDtypeStruct((blocks, step, inner), late.dtype),
        ]
        + [
            jax.ShapeDtypeStruct((count, step, width), late.dtype)
            for count in (1, blocks - 1, blocks)
        ],
        name="group_sums",
        compiler_params=pltpu.CompilerParams(vmem_limit_bytes=6 * MIB),
        cost_estimate=pl.CostEstimate(
            flops=2 * rows * width, bytes_accessed=6 * rows * width, transcendentals=0
        ),
    )(early, late)


def inverse_of(x):
    return lax.rsqrt(jnp.mean(x * x, axis=-1, keepdims=True) + EPSILON)


def unit_of(width, members, inner):
    return math.gcd(width // members, inner)


def write_normed(chips, x_ref, piece_refs):
    inverse = inverse_of(x_ref[...].astype(jnp.float32))
    unit = piece_refs[0].shape[-1]
    per_chip = x_ref.shape[1] // chips
    chip = lax.axis_index("dp") // 2
    for c, piece in enumerate(piece_refs):
        base = (chip ^ c) * per_chip
        for b in range(per_chip // unit):
            at = pl.ds(pl.multiple_of(base + b * unit, unit), unit)
            piece[b] = (x_ref[:, at].astype(jnp.float32) * inverse).astype(piece.dtype)


def arranged(match_ref, m, block_of, blocks):
    chosen = block_of(0).astype(jnp.float32)
    for j in range(1, blocks):
        mine = match_ref[m, j : j + 1, 0:1] != 0
        chosen = jnp.where(mine, block_of(j).astype(jnp.float32), chosen)
    return chosen


def write_grouped(at, value, own, grouped_ref, piece_refs):
    rows, inner = value.shape
    unit = piece_refs[0].shape[-1]
    grouped_ref[at : at + rows, :] = value
    for piece in piece_refs:
        for b in range(inner // unit):
            piece[own + b, at : at + rows, :] = value[:, b * unit : (b + 1) * unit]


def early_pieces_kernel(chips, x_ref, match_ref, sums_ref, grouped_ref, *pieces):
    write_normed(chips, x_ref, pieces)
    blocks, rows, _ = sums_ref.shape
    own = x_ref.shape[1] // chips // pieces[0].shape[-1]
    for m in range(blocks):
        value = arranged(match_ref, m, lambda j: sums_ref[j], blocks).astype(x_ref.dtype)
        write_grouped(m * rows, value, own, grouped_ref, pieces)


def late_pieces_kernel(
    chips, x_ref, match_ref, first_ref, rest_ref, sums_ref, grouped_ref, *pieces
):
    write_normed(chips, x_ref, pieces)
    half = first_ref.shape[1]
    blocks = match_ref.shape[0]
    own = x_ref.shape[1] // chips // pieces[0].shape[-1]
    raws = [(first_ref, 0)] + [(rest_ref, j) for j in range(blocks - 1)]
    firsts = []
    for ref, j in raws:
        sums = group_sum(lambda at: ref[j, :, at : at + HD])
        firsts.append(jnp.concatenate(sums, axis=-1).astype(x_ref.dtype))
    for part in range(2):
        for m in range(blocks):
            value = arranged(
                match_ref, m, lambda j: firsts[j] if part == 0 else sums_ref[j], blocks
            )
            at = (2 * m + part) * half
            write_grouped(at, value.astype(x_ref.dtype), own, grouped_ref, pieces)


def pieces_of(kernel, x, operands, inner, members):
    rows, width = x.shape
    chips = members // 2
    unit = unit_of(width, members, inner)
    count = width // chips // unit + inner // unit
    outputs = [jax.ShapeDtypeStruct((rows, inner), x.dtype)]
    outputs += [jax.ShapeDtypeStruct((count, rows, unit), x.dtype)] * chips
    return called(functools.partial(kernel, chips), (x, *operands), outputs, flops=4 * rows * width)


def product_kernel(chips, inner, *refs):
    early, late = refs[:chips], refs[chips : 2 * chips]
    keep_ref, send_ref = refs[2 * chips :]
    unit = early[0].shape[-1]
    half = keep_ref.shape[0] // unit
    own = 2 * half
    core = lax.axis_index("dp") % 2
    over_tokens = (((0,), (0,)), ((), ()))

    def stacked(at):
        return jnp.concatenate([ref[at] for ref in (*early, *late)], axis=0)

    for g in range(inner // unit):
        grouped = stacked(own + g)
        for dest, out_ref in ((core, keep_ref), (1 - core, send_ref)):
            for b in range(half):
                out_ref[b * unit : (b + 1) * unit, g * unit : (g + 1) * unit] = lax.dot_general(
                    stacked(dest * half + b),
                    grouped,
                    over_tokens,
                    preferred_element_type=jnp.float32,
                )


def products(early, late, width, inner, members):
    chips = members // 2
    rows = late[0].shape[1]
    out = jax.ShapeDtypeStruct((width // members, inner), jnp.float32)
    return called(
        functools.partial(product_kernel, chips, inner),
        (*early, *late),
        [out, out],
        flops=8 * chips * rows * (width // members) * inner,
        vmem=8,
    )


def combine_kernel(factor, keep_ref, got_ref, out_ref, held, sent):
    slots, step, _ = held.shape
    copies = []
    for i in range(slots):
        at = i * step
        held[i] = (keep_ref[at : at + step, :] + got_ref[at : at + step, :]) * factor
        copies.append(
            pltpu.make_async_copy(held.at[i], out_ref.at[pl.ds(at, step), :], sent.at[i])
        )
        copies[-1].start()
    for copy in copies:
        copy.wait()


def combined(keep, got, factor):
    rows, inner = keep.shape
    slots = 4
    return pl.pallas_call(
        functools.partial(combine_kernel, factor),
        in_specs=[whole_vmem()] * 2,
        out_specs=pl.BlockSpec(memory_space=pltpu.HBM),
        out_shape=jax.ShapeDtypeStruct(keep.shape, keep.dtype),
        scratch_shapes=[
            pltpu.VMEM((slots, rows // slots, inner), keep.dtype),
            pltpu.SemaphoreType.DMA((slots,)),
        ],
        name="combine",
        compiler_params=pltpu.CompilerParams(vmem_limit_bytes=4 * MIB),
        cost_estimate=pl.CostEstimate(
            flops=2 * rows * inner, bytes_accessed=12 * rows * inner, transcendentals=0
        ),
    )(keep, got)


def span_kernel(x_ref, grouped_ref, weight_ref, next_ref, through_ref, scaled, back, held, arrived):
    rows, width = x_ref.shape
    tiles, tile, inner = held.shape
    copies = [
        pltpu.make_async_copy(weight_ref.at[pl.ds(t * tile, tile), :], held.at[t], arrived.at[t])
        for t in range(tiles)
    ]
    for copy in copies:
        copy.start()
    x = x_ref[...].astype(jnp.float32)
    inverse = inverse_of(x)
    scaled[...] = x * inverse
    values = jnp.zeros((rows, inner), jnp.float32)
    total = jnp.zeros((rows, HD), jnp.float32)
    grouped = grouped_ref[...]
    for t, copy in enumerate(copies):
        copy.wait()
        weight = held[t]
        at = slice(t * tile, (t + 1) * tile)
        normed = scaled[:, at].astype(x_ref.dtype)
        values = values + jnp.dot(normed, weight, preferred_element_type=jnp.float32)
        part = lax.dot_general(
            grouped, weight, (((1,), (1,)), ((), ())), preferred_element_type=jnp.float32
        )
        back[:, at] = part
        for c in range(tile // HD):
            lanes = slice(c * HD, (c + 1) * HD)
            total = total + part[:, lanes] * scaled[:, t * tile + c * HD : t * tile + (c + 1) * HD]
    mean = jnp.sum(total, axis=-1, keepdims=True) * (1.0 / width)
    mean = jnp.broadcast_to(mean, (rows, HD))
    inverse = jnp.broadcast_to(inverse, (rows, HD))
    for k in range(KVH):
        spread = values[:, k * HD : (k + 1) * HD]
        for j in range(GROUPS):
            at = slice((k * GROUPS + j) * HD, (k * GROUPS + j + 1) * HD)
            next_ref[:, at] = (x_ref[:, at].astype(jnp.float32) + spread).astype(next_ref.dtype)
            through_ref[:, at] = inverse * (back[:, at] - scaled[:, at] * mean)


def span(x, grouped, weight):
    rows, width = x.shape
    inner = weight.shape[1]
    tile = math.gcd(width, 512)
    return called(
        span_kernel,
        (x, grouped, pltpu.with_memory_space_constraint(weight, pltpu.HBM)),
        [
            jax.ShapeDtypeStruct((rows, width), x.dtype),
            jax.ShapeDtypeStruct((rows, width), jnp.float32),
        ],
        scratch=[
            pltpu.VMEM((rows, width), jnp.float32),
            pltpu.VMEM((rows, width), jnp.float32),
            pltpu.VMEM((width // tile, tile, inner), weight.dtype),
            pltpu.SemaphoreType.DMA((width // tile,)),
        ],
        flops=4 * rows * width * inner,
        vmem=10,
        in_specs=[whole_vmem()] * 2 + [pl.BlockSpec(memory_space=pltpu.HBM)],
    )


def finish_kernel(parts, places, match_ref, through_ref, *refs):
    out_ref, held, sent = refs[-3:]
    blocks = match_ref.shape[0]
    half = held.shape[1]
    copies = []
    for i, part in enumerate(parts):

        def received(j):
            operand, at = places[i * blocks + j]
            return refs[operand][at].astype(jnp.float32)

        for m in range(blocks):
            chosen = received(0)
            for j in range(1, blocks):
                mine = match_ref[m, j : j + 1, 0:1] != 0
                chosen = jnp.where(mine, received(j), chosen)
            at = (2 * m + part) * half
            slot = i * blocks + m
            held[slot] = (chosen + through_ref[at : at + half, :]).astype(held.dtype)
            copies.append(
                pltpu.make_async_copy(
                    held.at[slot], out_ref.at[pl.ds(at, half), :], sent.at[slot]
                )
            )
            copies[-1].start()
    for copy in copies:
        copy.wait()


def finished(raws, parts, places, match, through, before=None):
    rows, width = through.shape
    blocks = match.shape[0]
    slots = blocks * len(parts)
    half = rows // blocks // 2
    operands = [match, through, *raws] + ([] if before is None else [before])
    specs = [whole_vmem()] * (2 + len(raws))
    if before is not None:
        specs.append(pl.BlockSpec(memory_space=pltpu.HBM))
    return pl.pallas_call(
        functools.partial(finish_kernel, parts, places),
        in_specs=specs,
        out_specs=pl.BlockSpec(memory_space=pltpu.HBM),
        out_shape=jax.ShapeDtypeStruct((rows, width), raws[0].dtype),
        scratch_shapes=[
            pltpu.VMEM((slots, half, width), raws[0].dtype),
            pltpu.SemaphoreType.DMA((slots,)),
        ],
        input_output_aliases={} if before is None else {len(operands) - 1: 0},
        name="finished",
        compiler_params=pltpu.CompilerParams(vmem_limit_bytes=4 * MIB),
        cost_estimate=pl.CostEstimate(
            flops=2 * slots * half * width,
            bytes_accessed=8 * slots * half * width,
            transcendentals=0,
        ),
    )(*operands)


def matches(roster_row):
    blocks = roster_row.shape[0]
    wanted = jnp.arange(blocks, dtype=jnp.int32)
    equal = (roster_row[None, :] == wanted[:, None]).astype(jnp.int32)
    return jnp.broadcast_to(equal[:, :, None], (blocks, blocks, HD))


def relayed(
    feed_early, feed_late, cotangent_early, cotangent_late, roster_early, roster_late, weight, by
):
    members = lax.axis_size("dp")
    chips = members // 2
    rows, width = feed_early.shape
    inner = weight.shape[1]
    match_early = matches(roster_early)
    match_late = matches(roster_late)

    sums_early, sums_late, *pieces = group_sums(
        cotangent_early, cotangent_late, roster_early.shape[0]
    )
    x_early = passed_along(feed_early, "section", by)
    sums_late = passed_along(sums_late, "section", by)
    sums_early = passed_along(sums_early, "section", -by)
    x_late = passed_along(feed_late, "section", -by)
    raw_late = [passed_along(piece, "section", by) for piece in pieces]
    raw_early = passed_along(cotangent_early, "section", -by)

    def exchanged(pieces):
        got = [pieces[0]]
        for c in range(1, chips):
            to = [(i, ((i // 2) ^ c) * 2 + i % 2) for i in range(members)]
            got.append(lax.ppermute(pieces[c], "dp", to))
        return got

    blocks = roster_early.shape[0]
    sums_early = sums_early.reshape(blocks, rows // blocks, inner)
    grouped_early, *sent_early = pieces_of(
        early_pieces_kernel, x_early, (match_early, sums_early), inner, members
    )
    got_early = exchanged(sent_early)
    grouped_late, *sent_late = pieces_of(
        late_pieces_kernel,
        x_late,
        (match_late, raw_late[0], raw_late[1], sums_late),
        inner,
        members,
    )
    got_late = exchanged(sent_late)

    next_early, through_early = span(x_early, grouped_early, weight)
    next_late, through_late = span(x_late, grouped_late, weight)

    keep, send = products(got_early, got_late, width, inner, members)
    got = lax.ppermute(send, "dp", [(i, i ^ 1) for i in range(members)])
    summed = combined(keep, got, float(2 * rows * members) ** (-0.5))

    raw_early = [raw_early.reshape(2 * blocks, rows // blocks // 2, width)]
    whole = [(0, 2 * j + part) for part in range(2) for j in range(blocks)]
    firsts = [(min(j, 1), max(j - 1, 0)) for j in range(blocks)]
    seconds = [(0, j) for j in range(blocks)]
    back_early = finished(raw_early, (0, 1), whole, match_early, through_early)
    part_late = finished(raw_late[:2], (0,), firsts, match_late, through_late)
    back_late = finished(raw_late[2:], (1,), seconds, match_late, through_late, part_late)
    return next_early, next_late, back_early, back_late, summed


def on_device(feed_down, feed_up, cotangent_down, cotangent_up, roster, value_weight):
    next_up, next_down, back_up, back_down, summed = relayed(
        feed_up[0],
        feed_down[0],
        cotangent_up[0],
        cotangent_down[0],
        roster[0, 1],
        roster[0, 0],
        value_weight[0],
        -1,
    )
    return (
        next_down[None],
        next_up[None],
        back_down[None],
        back_up[None],
        summed[None],
    )


def solution(mesh):
    rows = P("section", "dp", None)
    kept = P("section", None, None)
    return jax.shard_map(
        on_device,
        mesh=mesh,
        in_specs=(rows, rows, rows, rows, kept, kept),
        out_specs=(rows, rows, rows, rows, rows),
        check_vma=False,
    )
```

```python
import functools
import math

import jax
import jax.numpy as jnp
from jax import lax
from jax.experimental import pallas as pl
from jax.experimental.pallas import tpu as pltpu
from jax.sharding import PartitionSpec as P


KVH = 4
HD = 128
GROUPS = 8


EPSILON = 1e-05


MIB = 2**20


def passed_along(shard, axis, by):
    count = lax.axis_size(axis)
    return lax.ppermute(shard, axis, [(i, (i + by) % count) for i in range(count)])


def whole_vmem():
    return pl.BlockSpec(memory_space=pltpu.VMEM)


def called(kernel, operands, outputs, scratch=(), flops=0, vmem=4, **more):
    moved = sum(x.size * x.dtype.itemsize for x in list(operands) + list(outputs))
    return pl.pallas_call(
        kernel,
        in_specs=more.get("in_specs", [whole_vmem()] * len(operands)),
        out_specs=[whole_vmem()] * len(outputs),
        out_shape=list(outputs),
        scratch_shapes=list(scratch),
        compiler_params=pltpu.CompilerParams(vmem_limit_bytes=vmem * MIB),
        cost_estimate=pl.CostEstimate(
            flops=flops, bytes_accessed=moved, transcendentals=0
        ),
    )(*operands)


def group_sum(load):
    sums = []
    for k in range(KVH):
        total = load(k * GROUPS * HD).astype(jnp.float32)
        for j in range(1, GROUPS):
            total = total + load((k * GROUPS + j) * HD).astype(jnp.float32)
        sums.append(total)
    return sums


def group_kernel(
    early_ref, late_ref, early_out, late_out, first_out, rest_out, second_out
):
    block = pl.program_id(0)
    part = pl.program_id(1)
    for k, total in enumerate(group_sum(lambda at: early_ref[:, at : at + HD])):
        early_out[:, k * HD : (k + 1) * HD] = total.astype(early_out.dtype)

    @pl.when((part == 0) & (block == 0))
    def _():
        first_out[0] = late_ref[...]

    @pl.when((part == 0) & (block > 0))
    def _():
        rest_out[0] = late_ref[...]

    @pl.when(part == 1)
    def _():
        second_out[0] = late_ref[...]
        for k, total in enumerate(group_sum(lambda at: late_ref[:, at : at + HD])):
            late_out[0, :, k * HD : (k + 1) * HD] = total.astype(late_out.dtype)


def group_sums(early, late, blocks):
    rows, width = early.shape
    inner = width // GROUPS
    step = rows // blocks // 2
    wide = pl.BlockSpec((step, width), lambda j, i: (2 * j + i, 0))
    narrow = pl.BlockSpec((step, inner), lambda j, i: (2 * j + i, 0))
    later = pl.BlockSpec((1, step, inner), lambda j, i: (j, 0, 0))
    shape = (1, step, width)
    first = pl.BlockSpec(shape, lambda j, i: (0, 0, 0))
    rest = pl.BlockSpec(shape, lambda j, i: (jnp.maximum(j - 1, 0), 0, 0))
    second = pl.BlockSpec(shape, lambda j, i: (j, 0, 0))
    return pl.pallas_call(
        group_kernel,
        grid=(blocks, 2),
        in_specs=[wide, wide],
        out_specs=[narrow, later, first, rest, second],
        out_shape=[
            jax.ShapeDtypeStruct((rows, inner), early.dtype),
            jax.ShapeDtypeStruct((blocks, step, inner), late.dtype),
        ]
        + [
            jax.ShapeDtypeStruct((count, step, width), late.dtype)
            for count in (1, blocks - 1, blocks)
        ],
        name="group_sums",
        compiler_params=pltpu.CompilerParams(vmem_limit_bytes=6 * MIB),
        cost_estimate=pl.CostEstimate(
            flops=2 * rows * width, bytes_accessed=6 * rows * width, transcendentals=0
        ),
    )(early, late)


def inverse_of(x):
    return lax.rsqrt(jnp.mean(x * x, axis=-1, keepdims=True) + EPSILON)


def unit_of(width, members, inner):
    return math.gcd(width // members, inner)


def write_normed(chips, x_ref, piece_refs):
    inverse = inverse_of(x_ref[...].astype(jnp.float32))
    unit = piece_refs[0].shape[-1]
    per_chip = x_ref.shape[1] // chips
    chip = lax.axis_index("dp") // 2
    for c, piece in enumerate(piece_refs):
        base = (chip ^ c) * per_chip
        for b in range(per_chip // unit):
            at = pl.ds(pl.multiple_of(base + b * unit, unit), unit)
            piece[b] = (x_ref[:, at].astype(jnp.float32) * inverse).astype(piece.dtype)


def arranged(match_ref, m, block_of, blocks):
    chosen = block_of(0).astype(jnp.float32)
    for j in range(1, blocks):
        mine = match_ref[m, j : j + 1, 0:1] != 0
        chosen = jnp.where(mine, block_of(j).astype(jnp.float32), chosen)
    return chosen


def write_grouped(at, value, own, grouped_ref, piece_refs):
    rows, inner = value.shape
    unit = piece_refs[0].shape[-1]
    grouped_ref[at : at + rows, :] = value
    for piece in piece_refs:
        for b in range(inner // unit):
            piece[own + b, at : at + rows, :] = value[:, b * unit : (b + 1) * unit]


def early_pieces_kernel(chips, x_ref, match_ref, sums_ref, grouped_ref, *pieces):
    write_normed(chips, x_ref, pieces)
    blocks, rows, _ = sums_ref.shape
    own = x_ref.shape[1] // chips // pieces[0].shape[-1]
    for m in range(blocks):
        value = arranged(match_ref, m, lambda j: sums_ref[j], blocks).astype(x_ref.dtype)
        write_grouped(m * rows, value, own, grouped_ref, pieces)


def late_pieces_kernel(
    chips, x_ref, match_ref, first_ref, rest_ref, sums_ref, grouped_ref, *pieces
):
    write_normed(chips, x_ref, pieces)
    half = first_ref.shape[1]
    blocks = match_ref.shape[0]
    own = x_ref.shape[1] // chips // pieces[0].shape[-1]
    raws = [(first_ref, 0)] + [(rest_ref, j) for j in range(blocks - 1)]
    firsts = []
    for ref, j in raws:
        sums = group_sum(lambda at: ref[j, :, at : at + HD])
        firsts.append(jnp.concatenate(sums, axis=-1).astype(x_ref.dtype))
    for part in range(2):
        for m in range(blocks):
            value = arranged(
                match_ref, m, lambda j: firsts[j] if part == 0 else sums_ref[j], blocks
            )
            at = (2 * m + part) * half
            write_grouped(at, value.astype(x_ref.dtype), own, grouped_ref, pieces)


def pieces_of(kernel, x, operands, inner, members):
    rows, width = x.shape
    chips = members // 2
    unit = unit_of(width, members, inner)
    count = width // chips // unit + inner // unit
    outputs = [jax.ShapeDtypeStruct((rows, inner), x.dtype)]
    outputs += [jax.ShapeDtypeStruct((count, rows, unit), x.dtype)] * chips
    return called(functools.partial(kernel, chips), (x, *operands), outputs, flops=4 * rows * width)


def product_kernel(chips, inner, other, *refs):
    early, late = refs[:chips], refs[chips : 2 * chips]
    out_ref = refs[2 * chips]
    unit = early[0].shape[-1]
    half = out_ref.shape[0] // unit
    own = 2 * half
    core = lax.axis_index("dp") % 2
    dest = 1 - core if other else core
    over_tokens = (((0,), (0,)), ((), ()))

    def stacked(at):
        return jnp.concatenate([ref[at] for ref in (*early, *late)], axis=0)

    for g in range(inner // unit):
        grouped = stacked(own + g)
        for b in range(half):
            out_ref[b * unit : (b + 1) * unit, g * unit : (g + 1) * unit] = lax.dot_general(
                stacked(dest * half + b),
                grouped,
                over_tokens,
                preferred_element_type=jnp.float32,
            )


def products(early, late, width, inner, members, other):
    chips = members // 2
    rows = late[0].shape[1]
    (out,) = called(
        functools.partial(product_kernel, chips, inner, other),
        (*early, *late),
        [jax.ShapeDtypeStruct((width // members, inner), jnp.float32)],
        flops=4 * chips * rows * (width // members) * inner,
        vmem=8,
    )
    return out


def combine_kernel(factor, keep_ref, got_ref, out_ref, held, sent):
    slots, step, _ = held.shape
    copies = []
    for i in range(slots):
        at = i * step
        held[i] = (keep_ref[at : at + step, :] + got_ref[at : at + step, :]) * factor
        copies.append(
            pltpu.make_async_copy(held.at[i], out_ref.at[pl.ds(at, step), :], sent.at[i])
        )
        copies[-1].start()
    for copy in copies:
        copy.wait()


def combined(keep, got, factor):
    rows, inner = keep.shape
    slots = 4
    return pl.pallas_call(
        functools.partial(combine_kernel, factor),
        in_specs=[whole_vmem()] * 2,
        out_specs=pl.BlockSpec(memory_space=pltpu.HBM),
        out_shape=jax.ShapeDtypeStruct(keep.shape, keep.dtype),
        scratch_shapes=[
            pltpu.VMEM((slots, rows // slots, inner), keep.dtype),
            pltpu.SemaphoreType.DMA((slots,)),
        ],
        name="combine",
        compiler_params=pltpu.CompilerParams(vmem_limit_bytes=4 * MIB),
        cost_estimate=pl.CostEstimate(
            flops=2 * rows * inner, bytes_accessed=12 * rows * inner, transcendentals=0
        ),
    )(keep, got)


def span_kernel(x_ref, grouped_ref, weight_ref, next_ref, through_ref, scaled, back, held, arrived):
    rows, width = x_ref.shape
    tiles, tile, inner = held.shape
    copies = [
        pltpu.make_async_copy(weight_ref.at[pl.ds(t * tile, tile), :], held.at[t], arrived.at[t])
        for t in range(tiles)
    ]
    for copy in copies:
        copy.start()
    x = x_ref[...].astype(jnp.float32)
    inverse = inverse_of(x)
    scaled[...] = x * inverse
    values = jnp.zeros((rows, inner), jnp.float32)
    total = jnp.zeros((rows, HD), jnp.float32)
    grouped = grouped_ref[...]
    for t, copy in enumerate(copies):
        copy.wait()
        weight = held[t]
        at = slice(t * tile, (t + 1) * tile)
        normed = scaled[:, at].astype(x_ref.dtype)
        values = values + jnp.dot(normed, weight, preferred_element_type=jnp.float32)
        part = lax.dot_general(
            grouped, weight, (((1,), (1,)), ((), ())), preferred_element_type=jnp.float32
        )
        back[:, at] = part
        for c in range(tile // HD):
            lanes = slice(c * HD, (c + 1) * HD)
            total = total + part[:, lanes] * scaled[:, t * tile + c * HD : t * tile + (c + 1) * HD]
    mean = jnp.sum(total, axis=-1, keepdims=True) * (1.0 / width)
    mean = jnp.broadcast_to(mean, (rows, HD))
    inverse = jnp.broadcast_to(inverse, (rows, HD))
    for k in range(KVH):
        spread = values[:, k * HD : (k + 1) * HD]
        for j in range(GROUPS):
            at = slice((k * GROUPS + j) * HD, (k * GROUPS + j + 1) * HD)
            next_ref[:, at] = (x_ref[:, at].astype(jnp.float32) + spread).astype(next_ref.dtype)
            through_ref[:, at] = inverse * (back[:, at] - scaled[:, at] * mean)


def span(x, grouped, weight):
    rows, width = x.shape
    inner = weight.shape[1]
    tile = math.gcd(width, 512)
    return called(
        span_kernel,
        (x, grouped, pltpu.with_memory_space_constraint(weight, pltpu.HBM)),
        [
            jax.ShapeDtypeStruct((rows, width), x.dtype),
            jax.ShapeDtypeStruct((rows, width), jnp.float32),
        ],
        scratch=[
            pltpu.VMEM((rows, width), jnp.float32),
            pltpu.VMEM((rows, width), jnp.float32),
            pltpu.VMEM((width // tile, tile, inner), weight.dtype),
            pltpu.SemaphoreType.DMA((width // tile,)),
        ],
        flops=4 * rows * width * inner,
        vmem=10,
        in_specs=[whole_vmem()] * 2 + [pl.BlockSpec(memory_space=pltpu.HBM)],
    )


def finish_kernel(parts, places, match_ref, through_ref, *refs):
    out_ref, held, sent = refs[-3:]
    blocks = match_ref.shape[0]
    half = held.shape[1]
    copies = []
    for i, part in enumerate(parts):

        def received(j):
            operand, at = places[i * blocks + j]
            return refs[operand][at].astype(jnp.float32)

        for m in range(blocks):
            chosen = received(0)
            for j in range(1, blocks):
                mine = match_ref[m, j : j + 1, 0:1] != 0
                chosen = jnp.where(mine, received(j), chosen)
            at = (2 * m + part) * half
            slot = i * blocks + m
            held[slot] = (chosen + through_ref[at : at + half, :]).astype(held.dtype)
            copies.append(
                pltpu.make_async_copy(
                    held.at[slot], out_ref.at[pl.ds(at, half), :], sent.at[slot]
                )
            )
            copies[-1].start()
    for copy in copies:
        copy.wait()


def finished(raws, parts, places, match, through, before=None):
    rows, width = through.shape
    blocks = match.shape[0]
    slots = blocks * len(parts)
    half = rows // blocks // 2
    operands = [match, through, *raws] + ([] if before is None else [before])
    specs = [whole_vmem()] * (2 + len(raws))
    if before is not None:
        specs.append(pl.BlockSpec(memory_space=pltpu.HBM))
    return pl.pallas_call(
        functools.partial(finish_kernel, parts, places),
        in_specs=specs,
        out_specs=pl.BlockSpec(memory_space=pltpu.HBM),
        out_shape=jax.ShapeDtypeStruct((rows, width), raws[0].dtype),
        scratch_shapes=[
            pltpu.VMEM((slots, half, width), raws[0].dtype),
            pltpu.SemaphoreType.DMA((slots,)),
        ],
        input_output_aliases={} if before is None else {len(operands) - 1: 0},
        name="finished",
        compiler_params=pltpu.CompilerParams(vmem_limit_bytes=4 * MIB),
        cost_estimate=pl.CostEstimate(
            flops=2 * slots * half * width,
            bytes_accessed=8 * slots * half * width,
            transcendentals=0,
        ),
    )(*operands)


def matches(roster_row):
    blocks = roster_row.shape[0]
    wanted = jnp.arange(blocks, dtype=jnp.int32)
    equal = (roster_row[None, :] == wanted[:, None]).astype(jnp.int32)
    return jnp.broadcast_to(equal[:, :, None], (blocks, blocks, HD))


def relayed(
    feed_early, feed_late, cotangent_early, cotangent_late, roster_early, roster_late, weight, by
):
    members = lax.axis_size("dp")
    chips = members // 2
    rows, width = feed_early.shape
    inner = weight.shape[1]
    match_early = matches(roster_early)
    match_late = matches(roster_late)

    sums_early, sums_late, *pieces = group_sums(
        cotangent_early, cotangent_late, roster_early.shape[0]
    )
    x_early = passed_along(feed_early, "section", by)
    sums_late = passed_along(sums_late, "section", by)
    sums_early = passed_along(sums_early, "section", -by)
    x_late = passed_along(feed_late, "section", -by)
    raw_late = [passed_along(piece, "section", by) for piece in pieces]
    raw_early = passed_along(cotangent_early, "section", -by)

    def exchanged(pieces):
        got = [pieces[0]]
        for c in range(1, chips):
            to = [(i, ((i // 2) ^ c) * 2 + i % 2) for i in range(members)]
            got.append(lax.ppermute(pieces[c], "dp", to))
        return got

    blocks = roster_early.shape[0]
    sums_early = sums_early.reshape(blocks, rows // blocks, inner)
    grouped_early, *sent_early = pieces_of(
        early_pieces_kernel, x_early, (match_early, sums_early), inner, members
    )
    got_early = exchanged(sent_early)
    grouped_late, *sent_late = pieces_of(
        late_pieces_kernel,
        x_late,
        (match_late, raw_late[0], raw_late[1], sums_late),
        inner,
        members,
    )
    got_late = exchanged(sent_late)

    next_early, through_early = span(x_early, grouped_early, weight)
    next_late, through_late = span(x_late, grouped_late, weight)

    send = products(got_early, got_late, width, inner, members, True)
    keep = products(got_early, got_late, width, inner, members, False)
    got = lax.ppermute(send, "dp", [(i, i ^ 1) for i in range(members)])
    summed = combined(keep, got, float(2 * rows * members) ** (-0.5))

    raw_early = [raw_early.reshape(2 * blocks, rows // blocks // 2, width)]
    whole = [(0, 2 * j + part) for part in range(2) for j in range(blocks)]
    firsts = [(min(j, 1), max(j - 1, 0)) for j in range(blocks)]
    seconds = [(0, j) for j in range(blocks)]
    back_early = finished(raw_early, (0, 1), whole, match_early, through_early)
    part_late = finished(raw_late[:2], (0,), firsts, match_late, through_late)
    back_late = finished(raw_late[2:], (1,), seconds, match_late, through_late, part_late)
    return next_early, next_late, back_early, back_late, summed


def on_device(feed_down, feed_up, cotangent_down, cotangent_up, roster, value_weight):
    next_up, next_down, back_up, back_down, summed = relayed(
        feed_up[0],
        feed_down[0],
        cotangent_up[0],
        cotangent_down[0],
        roster[0, 1],
        roster[0, 0],
        value_weight[0],
        -1,
    )
    return (
        next_down[None],
        next_up[None],
        back_down[None],
        back_up[None],
        summed[None],
    )


def solution(mesh):
    rows = P("section", "dp", None)
    kept = P("section", None, None)
    return jax.shard_map(
        on_device,
        mesh=mesh,
        in_specs=(rows, rows, rows, rows, kept, kept),
        out_specs=(rows, rows, rows, rows, rows),
        check_vma=False,
    )
```

```python
import functools
import math

import jax
import jax.numpy as jnp
from jax import lax
from jax.experimental import pallas as pl
from jax.experimental.pallas import tpu as pltpu
from jax.sharding import PartitionSpec as P


KVH = 4
HD = 128
GROUPS = 8


EPSILON = 1e-05


MIB = 2**20


def passed_along(shard, axis, by):
    count = lax.axis_size(axis)
    return lax.ppermute(shard, axis, [(i, (i + by) % count) for i in range(count)])


def whole_vmem():
    return pl.BlockSpec(memory_space=pltpu.VMEM)


def called(kernel, operands, outputs, scratch=(), flops=0, vmem=4, **more):
    moved = sum(x.size * x.dtype.itemsize for x in list(operands) + list(outputs))
    return pl.pallas_call(
        kernel,
        in_specs=more.get("in_specs", [whole_vmem()] * len(operands)),
        out_specs=[whole_vmem()] * len(outputs),
        out_shape=list(outputs),
        scratch_shapes=list(scratch),
        compiler_params=pltpu.CompilerParams(vmem_limit_bytes=vmem * MIB),
        cost_estimate=pl.CostEstimate(
            flops=flops, bytes_accessed=moved, transcendentals=0
        ),
    )(*operands)


def group_sum(load):
    sums = []
    for k in range(KVH):
        total = load(k * GROUPS * HD).astype(jnp.float32)
        for j in range(1, GROUPS):
            total = total + load((k * GROUPS + j) * HD).astype(jnp.float32)
        sums.append(total)
    return sums


def group_kernel(
    early_ref, late_ref, early_out, late_out, first_out, rest_out, second_out
):
    block = pl.program_id(0)
    part = pl.program_id(1)
    for k, total in enumerate(group_sum(lambda at: early_ref[:, at : at + HD])):
        early_out[:, k * HD : (k + 1) * HD] = total.astype(early_out.dtype)

    @pl.when((part == 0) & (block == 0))
    def _():
        first_out[0] = late_ref[...]

    @pl.when((part == 0) & (block > 0))
    def _():
        rest_out[0] = late_ref[...]

    @pl.when(part == 1)
    def _():
        second_out[0] = late_ref[...]
        for k, total in enumerate(group_sum(lambda at: late_ref[:, at : at + HD])):
            late_out[0, :, k * HD : (k + 1) * HD] = total.astype(late_out.dtype)


def group_sums(early, late, blocks):
    rows, width = early.shape
    inner = width // GROUPS
    step = rows // blocks // 2
    wide = pl.BlockSpec((step, width), lambda j, i: (2 * j + i, 0))
    narrow = pl.BlockSpec((step, inner), lambda j, i: (2 * j + i, 0))
    later = pl.BlockSpec((1, step, inner), lambda j, i: (j, 0, 0))
    shape = (1, step, width)
    first = pl.BlockSpec(shape, lambda j, i: (0, 0, 0))
    rest = pl.BlockSpec(shape, lambda j, i: (jnp.maximum(j - 1, 0), 0, 0))
    second = pl.BlockSpec(shape, lambda j, i: (j, 0, 0))
    return pl.pallas_call(
        group_kernel,
        grid=(blocks, 2),
        in_specs=[wide, wide],
        out_specs=[narrow, later, first, rest, second],
        out_shape=[
            jax.ShapeDtypeStruct((rows, inner), early.dtype),
            jax.ShapeDtypeStruct((blocks, step, inner), late.dtype),
        ]
        + [
            jax.ShapeDtypeStruct((count, step, width), late.dtype)
            for count in (1, blocks - 1, blocks)
        ],
        name="group_sums",
        compiler_params=pltpu.CompilerParams(vmem_limit_bytes=6 * MIB),
        cost_estimate=pl.CostEstimate(
            flops=2 * rows * width, bytes_accessed=6 * rows * width, transcendentals=0
        ),
    )(
        pltpu.with_memory_space_constraint(early, pltpu.HBM),
        pltpu.with_memory_space_constraint(late, pltpu.HBM),
    )


def inverse_of(x):
    return lax.rsqrt(jnp.mean(x * x, axis=-1, keepdims=True) + EPSILON)


def unit_of(width, members, inner):
    return math.gcd(width // members, inner)


def write_normed(chips, x_ref, piece_refs):
    inverse = inverse_of(x_ref[...].astype(jnp.float32))
    unit = piece_refs[0].shape[-1]
    per_chip = x_ref.shape[1] // chips
    chip = lax.axis_index("dp") // 2
    for c, piece in enumerate(piece_refs):
        base = (chip ^ c) * per_chip
        for b in range(per_chip // unit):
            at = pl.ds(pl.multiple_of(base + b * unit, unit), unit)
            piece[b] = (x_ref[:, at].astype(jnp.float32) * inverse).astype(piece.dtype)


def arranged(match_ref, m, block_of, blocks):
    chosen = block_of(0).astype(jnp.float32)
    for j in range(1, blocks):
        mine = match_ref[m, j : j + 1, 0:1] != 0
        chosen = jnp.where(mine, block_of(j).astype(jnp.float32), chosen)
    return chosen


def write_grouped(at, value, own, grouped_ref, piece_refs):
    rows, inner = value.shape
    unit = piece_refs[0].shape[-1]
    grouped_ref[at : at + rows, :] = value
    for piece in piece_refs:
        for b in range(inner // unit):
            piece[own + b, at : at + rows, :] = value[:, b * unit : (b + 1) * unit]


def early_pieces_kernel(chips, x_ref, match_ref, sums_ref, grouped_ref, *pieces):
    write_normed(chips, x_ref, pieces)
    blocks, rows, _ = sums_ref.shape
    own = x_ref.shape[1] // chips // pieces[0].shape[-1]
    for m in range(blocks):
        value = arranged(match_ref, m, lambda j: sums_ref[j], blocks).astype(x_ref.dtype)
        write_grouped(m * rows, value, own, grouped_ref, pieces)


def late_pieces_kernel(
    chips, x_ref, match_ref, first_ref, rest_ref, sums_ref, grouped_ref, *pieces
):
    write_normed(chips, x_ref, pieces)
    half = first_ref.shape[1]
    blocks = match_ref.shape[0]
    own = x_ref.shape[1] // chips // pieces[0].shape[-1]
    raws = [(first_ref, 0)] + [(rest_ref, j) for j in range(blocks - 1)]
    firsts = []
    for ref, j in raws:
        sums = group_sum(lambda at: ref[j, :, at : at + HD])
        firsts.append(jnp.concatenate(sums, axis=-1).astype(x_ref.dtype))
    for part in range(2):
        for m in range(blocks):
            value = arranged(
                match_ref, m, lambda j: firsts[j] if part == 0 else sums_ref[j], blocks
            )
            at = (2 * m + part) * half
            write_grouped(at, value.astype(x_ref.dtype), own, grouped_ref, pieces)


def pieces_of(kernel, x, operands, inner, members):
    rows, width = x.shape
    chips = members // 2
    unit = unit_of(width, members, inner)
    count = width // chips // unit + inner // unit
    outputs = [jax.ShapeDtypeStruct((rows, inner), x.dtype)]
    outputs += [jax.ShapeDtypeStruct((count, rows, unit), x.dtype)] * chips
    return called(functools.partial(kernel, chips), (x, *operands), outputs, flops=4 * rows * width)


def product_kernel(chips, inner, other, *refs):
    early, late = refs[:chips], refs[chips : 2 * chips]
    out_ref = refs[2 * chips]
    unit = early[0].shape[-1]
    half = out_ref.shape[0] // unit
    own = 2 * half
    core = lax.axis_index("dp") % 2
    dest = 1 - core if other else core
    over_tokens = (((0,), (0,)), ((), ()))

    def stacked(at):
        return jnp.concatenate([ref[at] for ref in (*early, *late)], axis=0)

    for g in range(inner // unit):
        grouped = stacked(own + g)
        for b in range(half):
            out_ref[b * unit : (b + 1) * unit, g * unit : (g + 1) * unit] = lax.dot_general(
                stacked(dest * half + b),
                grouped,
                over_tokens,
                preferred_element_type=jnp.float32,
            )


def products(early, late, width, inner, members, other):
    chips = members // 2
    rows = late[0].shape[1]
    (out,) = called(
        functools.partial(product_kernel, chips, inner, other),
        (*early, *late),
        [jax.ShapeDtypeStruct((width // members, inner), jnp.float32)],
        flops=4 * chips * rows * (width // members) * inner,
        vmem=8,
    )
    return out


def combine_kernel(factor, keep_ref, got_ref, out_ref, held, sent):
    slots, step, _ = held.shape
    copies = []
    for i in range(slots):
        at = i * step
        held[i] = (keep_ref[at : at + step, :] + got_ref[at : at + step, :]) * factor
        copies.append(
            pltpu.make_async_copy(held.at[i], out_ref.at[pl.ds(at, step), :], sent.at[i])
        )
        copies[-1].start()
    for copy in copies:
        copy.wait()


def combined(keep, got, factor):
    rows, inner = keep.shape
    slots = 4
    return pl.pallas_call(
        functools.partial(combine_kernel, factor),
        in_specs=[whole_vmem()] * 2,
        out_specs=pl.BlockSpec(memory_space=pltpu.HBM),
        out_shape=jax.ShapeDtypeStruct(keep.shape, keep.dtype),
        scratch_shapes=[
            pltpu.VMEM((slots, rows // slots, inner), keep.dtype),
            pltpu.SemaphoreType.DMA((slots,)),
        ],
        name="combine",
        compiler_params=pltpu.CompilerParams(vmem_limit_bytes=4 * MIB),
        cost_estimate=pl.CostEstimate(
            flops=2 * rows * inner, bytes_accessed=12 * rows * inner, transcendentals=0
        ),
    )(keep, got)


def span_kernel(x_ref, grouped_ref, weight_ref, next_ref, through_ref, scaled, back, held, arrived):
    rows, width = x_ref.shape
    tiles, tile, inner = held.shape
    copies = [
        pltpu.make_async_copy(weight_ref.at[pl.ds(t * tile, tile), :], held.at[t], arrived.at[t])
        for t in range(tiles)
    ]
    for copy in copies:
        copy.start()
    x = x_ref[...].astype(jnp.float32)
    inverse = inverse_of(x)
    scaled[...] = x * inverse
    values = jnp.zeros((rows, inner), jnp.float32)
    total = jnp.zeros((rows, HD), jnp.float32)
    grouped = grouped_ref[...]
    for t, copy in enumerate(copies):
        copy.wait()
        weight = held[t]
        at = slice(t * tile, (t + 1) * tile)
        normed = scaled[:, at].astype(x_ref.dtype)
        values = values + jnp.dot(normed, weight, preferred_element_type=jnp.float32)
        part = lax.dot_general(
            grouped, weight, (((1,), (1,)), ((), ())), preferred_element_type=jnp.float32
        )
        back[:, at] = part
        for c in range(tile // HD):
            lanes = slice(c * HD, (c + 1) * HD)
            total = total + part[:, lanes] * scaled[:, t * tile + c * HD : t * tile + (c + 1) * HD]
    mean = jnp.sum(total, axis=-1, keepdims=True) * (1.0 / width)
    mean = jnp.broadcast_to(mean, (rows, HD))
    inverse = jnp.broadcast_to(inverse, (rows, HD))
    for k in range(KVH):
        spread = values[:, k * HD : (k + 1) * HD]
        for j in range(GROUPS):
            at = slice((k * GROUPS + j) * HD, (k * GROUPS + j + 1) * HD)
            next_ref[:, at] = (x_ref[:, at].astype(jnp.float32) + spread).astype(next_ref.dtype)
            through_ref[:, at] = inverse * (back[:, at] - scaled[:, at] * mean)


def span(x, grouped, weight):
    rows, width = x.shape
    inner = weight.shape[1]
    tile = math.gcd(width, 512)
    return called(
        span_kernel,
        (x, grouped, pltpu.with_memory_space_constraint(weight, pltpu.HBM)),
        [
            jax.ShapeDtypeStruct((rows, width), x.dtype),
            jax.ShapeDtypeStruct((rows, width), jnp.float32),
        ],
        scratch=[
            pltpu.VMEM((rows, width), jnp.float32),
            pltpu.VMEM((rows, width), jnp.float32),
            pltpu.VMEM((width // tile, tile, inner), weight.dtype),
            pltpu.SemaphoreType.DMA((width // tile,)),
        ],
        flops=4 * rows * width * inner,
        vmem=10,
        in_specs=[whole_vmem()] * 2 + [pl.BlockSpec(memory_space=pltpu.HBM)],
    )


def finish_kernel(parts, places, match_ref, through_ref, *refs):
    out_ref, held, sent = refs[-3:]
    blocks = match_ref.shape[0]
    half = held.shape[1]
    copies = []
    for i, part in enumerate(parts):

        def received(j):
            operand, at = places[i * blocks + j]
            return refs[operand][at].astype(jnp.float32)

        for m in range(blocks):
            chosen = received(0)
            for j in range(1, blocks):
                mine = match_ref[m, j : j + 1, 0:1] != 0
                chosen = jnp.where(mine, received(j), chosen)
            at = (2 * m + part) * half
            slot = i * blocks + m
            held[slot] = (chosen + through_ref[at : at + half, :]).astype(held.dtype)
            copies.append(
                pltpu.make_async_copy(
                    held.at[slot], out_ref.at[pl.ds(at, half), :], sent.at[slot]
                )
            )
            copies[-1].start()
    for copy in copies:
        copy.wait()


def finished(raws, parts, places, match, through, before=None):
    rows, width = through.shape
    blocks = match.shape[0]
    slots = blocks * len(parts)
    half = rows // blocks // 2
    operands = [match, through, *raws] + ([] if before is None else [before])
    specs = [whole_vmem()] * (2 + len(raws))
    if before is not None:
        specs.append(pl.BlockSpec(memory_space=pltpu.HBM))
    return pl.pallas_call(
        functools.partial(finish_kernel, parts, places),
        in_specs=specs,
        out_specs=pl.BlockSpec(memory_space=pltpu.HBM),
        out_shape=jax.ShapeDtypeStruct((rows, width), raws[0].dtype),
        scratch_shapes=[
            pltpu.VMEM((slots, half, width), raws[0].dtype),
            pltpu.SemaphoreType.DMA((slots,)),
        ],
        input_output_aliases={} if before is None else {len(operands) - 1: 0},
        name="finished",
        compiler_params=pltpu.CompilerParams(vmem_limit_bytes=4 * MIB),
        cost_estimate=pl.CostEstimate(
            flops=2 * slots * half * width,
            bytes_accessed=8 * slots * half * width,
            transcendentals=0,
        ),
    )(*operands)


def matches(roster_row):
    blocks = roster_row.shape[0]
    wanted = jnp.arange(blocks, dtype=jnp.int32)
    equal = (roster_row[None, :] == wanted[:, None]).astype(jnp.int32)
    return jnp.broadcast_to(equal[:, :, None], (blocks, blocks, HD))


def relayed(
    feed_early, feed_late, cotangent_early, cotangent_late, roster_early, roster_late, weight, by
):
    members = lax.axis_size("dp")
    chips = members // 2
    rows, width = feed_early.shape
    inner = weight.shape[1]
    match_early = matches(roster_early)
    match_late = matches(roster_late)

    sums_early, sums_late, *pieces = group_sums(
        cotangent_early, cotangent_late, roster_early.shape[0]
    )
    x_early = passed_along(feed_early, "section", by)
    sums_late = passed_along(sums_late, "section", by)
    sums_early = passed_along(sums_early, "section", -by)
    x_late = passed_along(feed_late, "section", -by)
    raw_late = [passed_along(piece, "section", by) for piece in pieces]
    raw_early = passed_along(cotangent_early, "section", -by)

    def exchanged(pieces):
        got = [pieces[0]]
        for c in range(1, chips):
            to = [(i, ((i // 2) ^ c) * 2 + i % 2) for i in range(members)]
            got.append(lax.ppermute(pieces[c], "dp", to))
        return got

    blocks = roster_early.shape[0]
    sums_early = sums_early.reshape(blocks, rows // blocks, inner)
    grouped_early, *sent_early = pieces_of(
        early_pieces_kernel, x_early, (match_early, sums_early), inner, members
    )
    got_early = exchanged(sent_early)
    grouped_late, *sent_late = pieces_of(
        late_pieces_kernel,
        x_late,
        (match_late, raw_late[0], raw_late[1], sums_late),
        inner,
        members,
    )
    got_late = exchanged(sent_late)

    next_early, through_early = span(x_early, grouped_early, weight)
    next_late, through_late = span(x_late, grouped_late, weight)

    send = products(got_early, got_late, width, inner, members, True)
    keep = products(got_early, got_late, width, inner, members, False)
    got = lax.ppermute(send, "dp", [(i, i ^ 1) for i in range(members)])
    summed = combined(keep, got, float(2 * rows * members) ** (-0.5))

    raw_early = [raw_early.reshape(2 * blocks, rows // blocks // 2, width)]
    whole = [(0, 2 * j + part) for part in range(2) for j in range(blocks)]
    firsts = [(min(j, 1), max(j - 1, 0)) for j in range(blocks)]
    seconds = [(0, j) for j in range(blocks)]
    back_early = finished(raw_early, (0, 1), whole, match_early, through_early)
    part_late = finished(raw_late[:2], (0,), firsts, match_late, through_late)
    back_late = finished(raw_late[2:], (1,), seconds, match_late, through_late, part_late)
    return next_early, next_late, back_early, back_late, summed


def on_device(feed_down, feed_up, cotangent_down, cotangent_up, roster, value_weight):
    next_up, next_down, back_up, back_down, summed = relayed(
        feed_up[0],
        feed_down[0],
        cotangent_up[0],
        cotangent_down[0],
        roster[0, 1],
        roster[0, 0],
        value_weight[0],
        -1,
    )
    return (
        next_down[None],
        next_up[None],
        back_down[None],
        back_up[None],
        summed[None],
    )


def solution(mesh):
    rows = P("section", "dp", None)
    kept = P("section", None, None)
    return jax.shard_map(
        on_device,
        mesh=mesh,
        in_specs=(rows, rows, rows, rows, kept, kept),
        out_specs=(rows, rows, rows, rows, rows),
        check_vma=False,
    )
```
